256 devices in a mesh: row: 64 (over z, x, core), col: 4 (over y).
Axes of the slice: x: 4, y: 4, z: 8, core: 2. Of those that a mesh axis runs over, the one named last changes fastest.
Arguments:
- right_sides: float32 [4, 256, 128, 128], P(None, 'row'), may hold values from -6 to 6
- inverse_diag: float32 [4, 256, 128, 128], P(None, 'row', 'col'), may hold values from -1 to 2
- lower_blocks: float32 [3, 256, 16, 128, 128], P(None, 'row', None, 'col'), may hold values from -0.09375 to 0.09375
- depends_on: int32 [3, 256, 16], replicated, may hold values from 0 to 255, as said below
Outputs:
- solution: float32 [4, 256, 128, 128], P(None, 'row', 'col')
The draws below stay inside these ranges and needn't reach their ends.
Inputs may be any that keep to these rules, and one draw needn't show every extreme that they name: `depends_on`: in each level, the supernodes of one device along row name the supernodes of any one device along row at most 2 times in all, and some pair of devices reaches 2 in every level.
All inputs are finite; a program needn't handle non-finite values.
Results may differ from the reference program's by a relative error of at most 0.0001.
Values sent between devices are 32-bit elements; how exact they have to be, the bound alone decides.
A program may use at most 64 MiB of HBM per device.

```python
import math
import jax
import jax.numpy as jnp
from jax import lax

S = 128
NRHS = 128
NB_DEV = 4
DEPS = 16
LEVELS = 4
NB = 256
CAP = 2


def draw_inverse_diag(key, part):
    first_key, second_key = jax.random.split(jax.random.fold_in(key, 11))
    noise = jnp.clip(jax.random.normal(first_key, (LEVELS, NB, S, S), jnp.float32), -5.0, 5.0) * (0.7 / math.sqrt(S))
    diagonal = jax.random.uniform(second_key, (LEVELS, NB, S), jnp.float32, 0.5, 1.5)
    identity = jnp.eye(S, dtype=jnp.float32)
    return jnp.tril(noise, -1) + diagonal[..., None] * identity


def draw_depends_on(key, part):
    entries = NB_DEV * DEPS
    devices = NB // NB_DEV
    tickets = devices * CAP

    def receiver(receiver_key):
        key_one, key_two, key_three, key_four = jax.random.split(receiver_key, 4)
        order = jax.random.permutation(key_one, tickets)
        focal = jax.random.randint(key_two, (), 0, devices)
        score = jnp.where(order // CAP == focal, 0, tickets) + jnp.arange(tickets)
        ranked = order[jnp.argsort(score)]
        chosen = ranked[:entries]
        chosen = chosen[jax.random.permutation(key_three, entries)]
        local_pick = jax.random.randint(key_four, (entries,), 0, NB_DEV)
        return chosen // CAP * NB_DEV + local_pick

    def one_level(level_key):
        return jax.vmap(receiver)(jax.random.split(level_key, devices)).reshape(NB, DEPS)
    level_keys = jax.random.split(jax.random.fold_in(key, 7), LEVELS - 1)
    return jax.vmap(one_level)(level_keys).astype(jnp.int32)


def steps_of(rng, extent, pieces, least, top_value):
    gain, own = 1.0, jax.random.fold_in(rng, 6)
    for position, parts in pieces:
        heights = jnp.exp(jax.random.uniform(jax.random.fold_in(own, position), (parts,), jnp.float32, least / len(pieces), top_value / len(pieces)))
        gain = gain * jnp.repeat(heights, extent[position] // parts).reshape([-1 if axis == position else 1 for axis in range(len(extent))])
    return gain


def centred(key, extent, spread, limit, cuts=(), kind=jnp.bfloat16):
    array = spread * jax.random.normal(key, extent, jnp.float32)
    if cuts:
        array = array * steps_of(key, extent, cuts, -0.22, 0.18)
    return jnp.clip(array, -limit, limit).astype(kind)


def setup_inputs(seed: int = 0) -> dict:
    keys = jax.random.split(jax.random.key(seed), 5)
    right_sides = centred(keys[0], (LEVELS, NB, S, NRHS), 1.0, 6.0, ((1, 64),), jnp.float32)
    inverse_diag = draw_inverse_diag(jax.random.fold_in(keys[4], 71), 0)
    lower_blocks = centred(keys[2], (LEVELS - 1, NB, DEPS, S, S), (2 * DEPS * S) ** -0.5, 0.09375, ((1, 64), (3, 4)), jnp.float32)
    depends_on = draw_depends_on(jax.random.fold_in(keys[4], 71), 0)
    return {"right_sides": right_sides, "inverse_diag": inverse_diag, "lower_blocks": lower_blocks, "depends_on": depends_on}


def reference(right_sides, inverse_diag, lower_blocks, depends_on):
    exact_mode = lax.Precision.HIGHEST
    current = jnp.einsum("jab,jbk->jak", inverse_diag[0], right_sides[0], precision=exact_mode)
    forward = [current]
    for level_no in range(1, LEVELS):
        picked = jnp.take(current, depends_on[level_no - 1], axis=0)
        update = jnp.einsum("jdba,jdbk->jak", lower_blocks[level_no - 1], picked, precision=exact_mode)
        current = jnp.einsum("jab,jbk->jak", inverse_diag[level_no], right_sides[level_no] - update, precision=exact_mode)
        forward.append(current)
    upper_sol = jnp.einsum("jab,jak->jbk", inverse_diag[LEVELS - 1], forward[LEVELS - 1], precision=exact_mode)
    solved = [upper_sol]
    for level_no in range(LEVELS - 2, -1, -1):
        contrib = jnp.einsum("jdba,jak->jdbk", lower_blocks[level_no], upper_sol, precision=exact_mode)
        returned = jax.ops.segment_sum(contrib.reshape(NB * DEPS, S, NRHS), depends_on[level_no].reshape(NB * DEPS), num_segments=NB)
        upper_sol = jnp.einsum("jab,jak->jbk", inverse_diag[level_no], forward[level_no] - returned, precision=exact_mode)
        solved.insert(0, upper_sol)
    return jnp.stack(solved)
```

```python
import jax
import jax.numpy as jnp
from jax import lax
from jax.experimental import pallas as pl
from jax.experimental.pallas import tpu as pltpu
from jax.sharding import PartitionSpec as P

MESH = pl.DeviceIdType.MESH
EXACT = lax.Precision.HIGHEST
NZ, NX = 8, 4
X_POS = {0: 0, 1: 1, 3: 2, 2: 3}
Z_POS = {0: 0, 1: 1, 7: 2, 2: 3, 6: 4, 3: 5, 5: 6, 4: 7}
GROUPS = [(0, 1), (1, 2), (3, 2), (5, 2), (7, 1)]


def exact_dot(a, b):
    return jnp.dot(a, b, precision=EXACT, preferred_element_type=jnp.float32)


def ring_pos(distance, size):
    return jnp.where(
        distance == 0,
        0,
        jnp.where(distance <= size // 2, 2 * distance - 1, 2 * (size - distance)),
    )


def block_place(block, z_of, x_of):
    owner, local = block // 4, block % 4
    a = z_of(owner // (2 * NX)) % NZ
    b = x_of(owner // 2 % NX) % NX
    slot_a = a * NX + ring_pos(b, NX)
    slot_b = ring_pos(b, NX) * NZ + ring_pos(a, NZ)
    return jnp.where(local < 2, 2 * slot_a, 64 + 2 * slot_b) + local % 2, owner % 2


def kernel(
    fwd_idx, bwd_idx, rhs_hbm, inv_hbm, low_hbm, out_ref,
    rhs, inv, low, low_t, fwd, own_part, gath_0, gath_1, gath_2, part, col_in, rest,
    sol, terms_0, terms_1, terms_2, own, up_a, dn_a, row_x, in_x, mid_l, mid_r, fin_l, fin_r, col_z, up_z, dn_z,
    load_sem, send_sem, inv_sem, ag_sem, rs_sem, col_sem,
):
    gath, terms = (gath_0, gath_1, gath_2), (terms_0, terms_1, terms_2)
    row, c = lax.axis_index("row"), lax.axis_index("col")
    z, x, core = row // (2 * NX), row // 2 % NX, row % 2

    def at_row(zz, xx, cc):
        return ((zz * NX + xx) * 2 + cc, c)

    z_up, z_dn = at_row((z + 1) % NZ, x, core), at_row((z + NZ - 1) % NZ, x, core)
    x_rt, x_lf = at_row(z, (x + 1) % NX, core), at_row(z, (x + NX - 1) % NX, core)
    x_far = at_row(z, (x + 2) % NX, core)
    sib = at_row(z, x, 1 - core)
    col_dev = [None] + [(row, (c + t) % 4) for t in (1, 2, 3)]

    loads = [
        pltpu.make_async_copy(inv_hbm, inv.at[:, :, c], load_sem.at[0]),
        pltpu.make_async_copy(rhs_hbm.at[0], rhs.at[0], load_sem.at[1]),
        pltpu.make_async_copy(rhs_hbm.at[pl.ds(1, 3)], rhs.at[pl.ds(1, 3)], load_sem.at[2]),
        pltpu.make_async_copy(low_hbm, low, load_sem.at[3]),
    ]
    for load in loads:
        load.start()

    barrier = pltpu.get_barrier_semaphore()
    partners = [z_up, z_dn, x_rt, x_lf, x_far, sib] + col_dev[1:]
    for partner in partners:
        pl.semaphore_signal(barrier, inc=1, device_id=partner, device_id_type=MESH)

    for level in range(3):
        terms[level][128] = jnp.zeros((32, 128), jnp.float32)
    loads[0].wait()
    loads[1].wait()
    for j in range(4):
        fwd[0, j] = exact_dot(inv[0, j, c], rhs[0, j])
    pl.semaphore_wait(barrier, len(partners))

    def put(src, dst, sem, device, out_sem):
        pltpu.make_async_remote_copy(
            src_ref=src, dst_ref=dst, send_sem=out_sem, recv_sem=sem, device_id=device, device_id_type=MESH
        ).start()

    def take(dst, sem, device=None):
        pltpu.make_async_remote_copy(
            src_ref=dst, dst_ref=dst, send_sem=send_sem.at[0], recv_sem=sem, device_id=sib, device_id_type=MESH
        ).wait_recv()

    def sent(count, out_sem):
        ref = gath[0].at[pl.ds(0, count)]
        pltpu.make_async_remote_copy(
            src_ref=ref, dst_ref=ref, send_sem=out_sem, recv_sem=out_sem, device_id=sib, device_id_type=MESH
        ).wait_send()

    def gather_row(level, between):
        g_sem = send_sem.at[0]
        ids = {}

        def sem(key):
            return ag_sem.at[level, ids.setdefault(key, len(ids))]

        def ref_a(a, pos, count):
            return gath[level].at[pl.ds(2 * (a * NX + pos), 2 * count)]

        def ref_b(pos, zpos, count):
            return gath[level].at[pl.ds(64 + 2 * (pos * NZ + zpos), 2 * count)]

        sib_sem = sem("sib")

        def share(first, count):
            put(
                gath[level].at[pl.ds(first, count)], gath[level].at[pl.ds(128 + first, count)],
                sib_sem, sib, g_sem,
            )

        def share_a(a, pos, count):
            share(2 * (a * NX + pos), 2 * count)

        def share_b(pos, zpos, count):
            share(64 + 2 * (pos * NZ + zpos), 2 * count)

        def z_a(a, p, direction):
            to = (a + direction) % NZ
            put(
                ref_a(a, 2 * p, 2), ref_a(to, 2 * p, 2), sem(("az", to, p)),
                z_up if direction == 1 else z_dn, g_sem,
            )

        def z_b(a, direction):
            to = (a + direction) % NZ
            put(
                ref_b(0, Z_POS[a], 1), ref_b(0, Z_POS[to], 1), sem(("bz", to)),
                z_up if direction == 1 else z_dn, g_sem,
            )

        def x_b(group):
            zpos, count = GROUPS[group]
            put(ref_b(0, zpos, count), ref_b(1, zpos, count), sem(("bl", group)), x_rt, g_sem)
            put(ref_b(0, zpos, count), ref_b(2, zpos, count), sem(("br", group)), x_lf, g_sem)

        def far_b(group):
            zpos, count = GROUPS[group]
            if group in (0, 1, 4):
                put(ref_b(1, zpos, count), ref_b(3, zpos, count), sem(("b2", group)), x_rt, g_sem)
            else:
                put(ref_b(2, zpos, count), ref_b(3, zpos, count), sem(("b2", group)), x_lf, g_sem)

        def got_x_b(group):
            zpos, count = GROUPS[group]
            if group in (0, 1, 4):
                take(ref_b(1, zpos, count), sem(("bl", group)))
                far_b(group)
                take(ref_b(2, zpos, count), sem(("br", group)))
            else:
                take(ref_b(2, zpos, count), sem(("br", group)))
                far_b(group)
                take(ref_b(1, zpos, count), sem(("bl", group)))
            share_b(1, zpos, count)
            share_b(2, zpos, count)

        def got_z_b(a):
            take(ref_b(0, Z_POS[a], 1), sem(("bz", a)))

        def got_z_a(a, p):
            take(ref_a(a, 2 * p, 2), sem(("az", a, p)))

        gath[level][pl.ds(0, 2)] = fwd[level, pl.ds(0, 2)]
        gath[level][pl.ds(64, 2)] = fwd[level, pl.ds(2, 2)]
        z_b(0, 1)
        z_b(0, -1)
        put(ref_a(0, 0, 1), ref_a(0, 1, 1), sem("ax1"), x_rt, g_sem)
        put(ref_a(0, 0, 1), ref_a(0, 2, 1), sem("ax3"), x_lf, g_sem)
        put(ref_a(0, 0, 1), ref_a(0, 3, 1), sem("ax2"), x_far, g_sem)
        x_b(0)
        share_a(0, 0, 1)
        share_b(0, 0, 1)
        between()
        take(ref_a(0, 1, 1), sem("ax1"))
        z_a(0, 0, 1)
        z_a(0, 0, -1)
        got_z_b(1)
        z_b(1, 1)
        got_z_b(7)
        z_b(7, -1)
        x_b(1)
        take(ref_a(0, 2, 1), sem("ax3"))
        take(ref_a(0, 3, 1), sem("ax2"))
        z_a(0, 1, 1)
        z_a(0, 1, -1)
        share_a(0, 1, 3)
        share_b(0, 1, 2)
        got_x_b(0)
        got_z_b(2)
        z_b(2, 1)
        got_z_b(6)
        z_b(6, -1)
        x_b(2)
        got_z_a(1, 0)
        z_a(1, 0, 1)
        got_z_a(7, 0)
        z_a(7, 0, -1)
        got_z_a(1, 1)
        z_a(1, 1, 1)
        got_z_a(7, 1)
        z_a(7, 1, -1)
        share_a(1, 0, 4)
        share_a(7, 0, 4)
        share_b(0, 3, 2)
        got_x_b(1)
        got_z_b(3)
        z_b(3, 1)
        got_z_b(5)
        x_b(3)
        got_z_a(2, 0)
        z_a(2, 0, 1)
        got_z_a(6, 0)
        z_a(6, 0, -1)
        got_z_a(2, 1)
        z_a(2, 1, 1)
        got_z_a(6, 1)
        z_a(6, 1, -1)
        share_a(2, 0, 4)
        share_a(6, 0, 4)
        share_b(0, 5, 2)
        got_x_b(2)
        got_z_b(4)
        x_b(4)
        share_b(0, 7, 1)
        got_x_b(3)
        got_z_a(3, 0)
        z_a(3, 0, 1)
        got_z_a(5, 1)
        z_a(5, 1, -1)
        got_z_a(3, 1)
        got_z_a(5, 0)
        share_a(3, 0, 4)
        share_a(5, 0, 4)
        got_x_b(4)
        for group in range(5):
            zpos, count = GROUPS[group]
            take(ref_b(3, zpos, count), sem(("b2", group)))
        share_b(3, 0, 8)
        got_z_a(4, 0)
        got_z_a(4, 1)
        share_a(4, 0, 4)
        take(gath[level].at[pl.ds(128, 128)], sib_sem)
        sent(252, g_sem)

    def reduce_row(low_level):
        r_sem = send_sem.at[0]
        ids = {}

        def sem(key):
            return rs_sem.at[low_level, ids.setdefault(key, len(ids))]

        def own_a(a, p):
            return own.at[low_level, pl.ds(2 * (a * NX + 2 * p), 4)]

        def own_b(pos, zpos, count):
            return own.at[low_level, pl.ds(64 + 2 * (pos * NZ + zpos), 2 * count)]

        def ref_az(a, p, direction):
            buffer, slot = (up_a, a) if direction == 1 else (dn_a, (NZ - a) % NZ)
            return buffer.at[low_level, slot, p]

        def send_az(src, a, p, direction):
            to = a - direction if direction == 1 else a + 1
            to = to % NZ
            put(
                src, ref_az(to, p, direction), sem(("az", to, p, direction)),
                z_up if direction == 1 else z_dn, r_sem,
            )

        def pass_az(a, p, direction):
            ref = ref_az(a, p, direction)
            take(ref, sem(("az", a, p, direction)))
            if a:
                ref[...] += own_a(a, p)[...]
                send_az(ref, a, p, direction)

        zs = [(7, 1), (3, 4), (0, 3)]

        def mid(buffer, part_no):
            zpos, count = zs[part_no]
            return buffer.at[low_level, pl.ds(2 * zpos, 2 * count)]

        put(own_b(3, 7, 1), mid(mid_l, 0), sem(("m", 0)), x_rt, r_sem)
        put(own_b(2, 7, 1), mid(fin_r, 0), sem(("fr", 0)), x_lf, r_sem)
        send_az(own_a(4, 0), 4, 0, 1)
        send_az(own_a(4, 1), 4, 1, -1)
        put(own_b(3, 3, 4), mid(mid_r, 1), sem(("m", 1)), x_lf, r_sem)
        put(own_b(3, 0, 3), mid(mid_l, 2), sem(("m", 2)), x_rt, r_sem)
        send_az(own_a(3, 1), 3, 1, 1)
        send_az(own_a(5, 0), 5, 0, -1)
        put(own_b(1, 3, 4), mid(fin_l, 1), sem(("fl", 1)), x_rt, r_sem)
        put(own_b(2, 0, 3), mid(fin_r, 2), sem(("fr", 2)), x_lf, r_sem)

        take(mid(mid_l, 0), sem(("m", 0)))
        mid(mid_l, 0)[...] += own_b(1, 7, 1)[...]
        put(mid(mid_l, 0), mid(fin_l, 0), sem(("fl", 0)), x_rt, r_sem)
        pass_az(3, 0, 1)
        pass_az(5, 1, -1)
        take(mid(mid_r, 1), sem(("m", 1)))
        mid(mid_r, 1)[...] += own_b(2, 3, 4)[...]
        put(mid(mid_r, 1), mid(fin_r, 1), sem(("fr", 1)), x_lf, r_sem)
        pass_az(2, 1, 1)
        pass_az(6, 0, -1)
        take(mid(mid_l, 2), sem(("m", 2)))
        mid(mid_l, 2)[...] += own_b(1, 0, 3)[...]
        put(mid(mid_l, 2), mid(fin_l, 2), sem(("fl", 2)), x_rt, r_sem)

        def ref_bz(a, direction):
            buffer, slot = (up_z, a) if direction == 1 else (dn_z, (NZ - a) % NZ)
            return buffer.at[low_level, slot]

        def send_bz(src, a, direction):
            to = (a - 1 if direction == 1 else a + 1) % NZ
            put(
                src, ref_bz(to, direction), sem(("bz", to, direction)),
                z_up if direction == 1 else z_dn, r_sem,
            )

        def pass_bz(a, direction):
            ref = ref_bz(a, direction)
            take(ref, sem(("bz", a, direction)))
            if a:
                ref[...] += col_z[low_level, pl.ds(2 * Z_POS[a], 2)]
                send_bz(ref, a, direction)

        def finish_x(part_no):
            zpos, count = zs[part_no]
            take(mid(fin_l, part_no), sem(("fl", part_no)))
            take(mid(fin_r, part_no), sem(("fr", part_no)))
            col_z[low_level, pl.ds(2 * zpos, 2 * count)] = (
                own_b(0, zpos, count)[...] + mid(fin_l, part_no)[...] + mid(fin_r, part_no)[...]
            )

        def col_at(a):
            return col_z.at[low_level, pl.ds(2 * Z_POS[a], 2)]

        finish_x(0)
        send_bz(col_at(4), 4, 1)
        pass_az(2, 0, 1)
        pass_az(6, 1, -1)
        finish_x(1)
        send_bz(col_at(5), 5, -1)
        pass_bz(3, 1)
        pass_az(1, 1, 1)
        pass_az(7, 0, -1)
        pass_bz(6, -1)
        pass_bz(2, 1)
        finish_x(2)
        pass_az(1, 0, 1)
        pass_az(7, 1, -1)
        pass_bz(7, -1)
        pass_bz(1, 1)
        for p in (1, 0):
            pass_az(0, p, 1)
            pass_az(0, p, -1)
            row_x[low_level, p] = own_a(0, p)[...] + up_a[low_level, 0, p] + dn_a[low_level, 0, p]
            if p == 1:
                put(row_x.at[low_level, 1, pl.ds(2, 2)], in_x.at[low_level, 2], sem("x3"), x_far, r_sem)
                put(row_x.at[low_level, 1, pl.ds(0, 2)], in_x.at[low_level, 1], sem("x2"), x_lf, r_sem)
            else:
                put(row_x.at[low_level, 0, pl.ds(2, 2)], in_x.at[low_level, 0], sem("x1"), x_rt, r_sem)
        pass_bz(0, -1)
        pass_bz(0, 1)
        half_b = col_z[low_level, pl.ds(0, 2)] + up_z[low_level, 0] + dn_z[low_level, 0]
        for slot in (2, 1, 0):
            take(in_x.at[low_level, slot], sem("x%d" % (slot + 1)))
        half_a = (
            row_x[low_level, 0, pl.ds(0, 2)] + in_x[low_level, 0] + in_x[low_level, 1] + in_x[low_level, 2]
        )
        sent(188, r_sem)
        return half_a, half_b

    for level in (1, 2, 3, 0):
        for t in (1, 2, 3):
            ref = inv.at[level, :, c]
            put(ref, ref, inv_sem.at[level, t - 1], col_dev[t], send_sem.at[1])

    def whole_inv(level):
        for t in (1, 2, 3):
            take(inv.at[level, :, 0], inv_sem.at[level, t - 1])

    def forward_level(low_level):
        level = low_level + 1

        def between():
            if low_level == 0:
                loads[2].wait()
                loads[3].wait()

            for j in range(4):
                own_part[j] = exact_dot(inv[level, j, c], rhs[level, j])
            for j in range(4):
                low_t[j] = low[low_level, j].T

        gather_row(low_level, between)
        whole_inv(level)
        for j in range(4):
            picked = jnp.concatenate([gath[low_level][fwd_idx[low_level, 16 * j + d]] for d in range(16)], axis=0)
            update = exact_dot(low_t[j], picked)
            done = exact_dot(inv[level, j].reshape(128, 128), update)
            for piece in range(4):
                part[low_level, piece, j] = done[32 * piece : 32 * piece + 32]
        for t in (1, 2, 3):
            put(
                part.at[low_level, (c + t) % 4], col_in.at[low_level, t - 1],
                col_sem.at[low_level, t - 1], col_dev[t], send_sem.at[0],
            )
        for t in (1, 2, 3):
            take(col_in.at[low_level, t - 1], col_sem.at[low_level, t - 1])
        fwd[level] = (
            own_part[...] - part[low_level, c]
            - col_in[low_level, 0] - col_in[low_level, 1] - col_in[low_level, 2]
        )
        sent(12, send_sem.at[0])

    for low_level in range(3):
        forward_level(low_level)
    whole_inv(0)

    def solve_level(level):
        ref = rest.at[level, c]
        for t in (1, 2, 3):
            put(ref, ref, col_sem.at[3 + level, t - 1], col_dev[t], send_sem.at[0])
        for t in (1, 2, 3):
            take(ref, col_sem.at[3 + level, t - 1])
        for j in range(4):
            whole = inv[level, j].reshape(128, 128)
            sol[j] = exact_dot(whole.T, rest[level, :, j].reshape(128, 128))
        for j in range(4):
            out_ref[level, j] = sol[j, pl.ds(pl.multiple_of(32 * c, 32), 32), :]
        sent(12, send_sem.at[0])

    rest[3, c] = fwd[3]

    def backward_level(low_level):
        solve_level(low_level + 1)
        t_sem = rs_sem.at[low_level, 63]
        for j in range(4):
            product = exact_dot(low[low_level, j], sol[j])
            terms[low_level][pl.ds(16 * j, 16)] = product.reshape(16, 32, 128)
            put(
                terms[low_level].at[pl.ds(16 * j, 16)], terms[low_level].at[pl.ds(64 + 16 * j, 16)],
                t_sem, sib, send_sem.at[0],
            )
        take(terms[low_level].at[pl.ds(64, 64)], t_sem)

        def build(place, inner):
            own[low_level, place] = (
                terms[low_level][bwd_idx[low_level, 4 * place]]
                + terms[low_level][bwd_idx[low_level, 4 * place + 1]]
                + terms[low_level][bwd_idx[low_level, 4 * place + 2]]
                + terms[low_level][bwd_idx[low_level, 4 * place + 3]]
            )
            return inner

        lax.fori_loop(0, 128, build, 0)
        half_a, half_b = reduce_row(low_level)
        rest[low_level, c, pl.ds(0, 2)] = fwd[low_level, pl.ds(0, 2)] - half_a
        rest[low_level, c, pl.ds(2, 2)] = fwd[low_level, pl.ds(2, 2)] - half_b

    for low_level in (2, 1, 0):
        backward_level(low_level)
    solve_level(0)
    sent(48, send_sem.at[1])


def on_device(right_sides, inverse_diag, lower_blocks, depends_on):
    row = lax.axis_index("row")
    z, x, core = row // (2 * NX), row // 2 % NX, row % 2
    mine = lax.dynamic_slice(depends_on, (0, 4 * row, 0), (3, 4, 16)).reshape(3, 64)
    other = lax.dynamic_slice(depends_on, (0, 4 * (row + 1 - 2 * core), 0), (3, 4, 16)).reshape(3, 64)
    place, owner_core = block_place(mine, lambda zz: z - zz, lambda xx: x - xx)
    fwd_idx = place + jnp.where(owner_core == core, 0, 128)
    lists = []
    for base, wanted in ((0, mine), (64, other)):
        place, owner_core = block_place(wanted, lambda zz: zz - z, lambda xx: xx - x)
        place = jnp.where(owner_core == core, place, -1)
        match = place[:, None, :] == jnp.arange(128, dtype=jnp.int32)[None, :, None]
        entry = jnp.arange(64, dtype=jnp.int32)[None, None, :]
        first = jnp.min(jnp.where(match, entry, 64), axis=2)
        last = jnp.max(jnp.where(match, entry, -1), axis=2)
        lists.append(jnp.where(first == 64, 128, base + first))
        lists.append(jnp.where(last > first, base + last, 128))
    bwd_idx = jnp.stack(lists, axis=2).reshape(3, 512)

    f32 = jnp.float32

    def vmem(*shape):
        return pltpu.VMEM(shape, f32)

    any_spec = pl.BlockSpec(memory_space=pl.ANY)
    smem_spec = pl.BlockSpec(memory_space=pltpu.SMEM)
    block = (32, 128)
    return pl.pallas_call(
        kernel,
        out_shape=jax.ShapeDtypeStruct((4, 4, 32, 128), f32),
        in_specs=[smem_spec, smem_spec, any_spec, any_spec, any_spec],
        out_specs=pl.BlockSpec(memory_space=pltpu.VMEM),
        scratch_shapes=[
            vmem(4, 4, 128, 128),
            vmem(4, 4, 4, *block),
            vmem(3, 4, 512, 128),
            vmem(4, 128, 512),
            vmem(4, 4, *block),
            vmem(4, *block),
            vmem(256, *block),
            vmem(256, *block),
            vmem(256, *block),
            vmem(3, 4, 4, *block),
            vmem(3, 3, 4, *block),
            vmem(4, 4, 4, *block),
            vmem(4, 128, 128),
            vmem(129, *block),
            vmem(129, *block),
            vmem(129, *block),
            vmem(3, 128, *block),
            vmem(3, 4, 2, 4, *block),
            vmem(3, 4, 2, 4, *block),
            vmem(3, 2, 4, *block),
            vmem(3, 3, 2, *block),
            vmem(3, 16, *block),
            vmem(3, 16, *block),
            vmem(3, 16, *block),
            vmem(3, 16, *block),
            vmem(3, 16, *block),
            vmem(3, 4, 2, *block),
            vmem(3, 4, 2, *block),
            pltpu.SemaphoreType.DMA((4,)),
            pltpu.SemaphoreType.DMA((2,)),
            pltpu.SemaphoreType.DMA((4, 3)),
            pltpu.SemaphoreType.DMA((3, 64)),
            pltpu.SemaphoreType.DMA((3, 64)),
            pltpu.SemaphoreType.DMA((7, 3)),
        ],
        compiler_params=pltpu.CompilerParams(
            collective_id=0, has_side_effects=True, vmem_limit_bytes=60 * 1024 * 1024
        ),
    )(fwd_idx, bwd_idx, right_sides, inverse_diag, lower_blocks.reshape(3, 4, 512, 128))


def solution(mesh):
    return jax.shard_map(
        on_device,
        mesh=mesh,
        in_specs=(
            P(None, "row", None, None),
            P(None, "row", "col", None),
            P(None, "row", None, "col", None),
            P(),
        ),
        out_specs=P(None, "row", "col", None),
        check_vma=False,
    )
```

```python
import jax
import jax.numpy as jnp
from jax import lax
from jax.experimental import pallas as pl
from jax.experimental.pallas import tpu as pltpu
from jax.sharding import PartitionSpec as P

MESH = pl.DeviceIdType.MESH
NZ, NX = 8, 4
X_POS = {0: 0, 1: 1, 3: 2, 2: 3}
Z_POS = {0: 0, 1: 1, 7: 2, 2: 3, 6: 4, 3: 5, 5: 6, 4: 7}
GROUPS = [(0, 1), (1, 2), (3, 2), (5, 2), (7, 1)]


def split(v):
    high = v.astype(jnp.bfloat16)
    return high, (v - high.astype(jnp.float32)).astype(jnp.bfloat16)


def split_dot(a, b):
    def dot(u, v):
        return jnp.dot(u, v, preferred_element_type=jnp.float32)

    return dot(a[0], b[0]) + (dot(a[0], b[1]) + dot(a[1], b[0]))


def exact_dot(a, b):
    return split_dot(split(a), split(b))


def ring_pos(distance, size):
    return jnp.where(
        distance == 0,
        0,
        jnp.where(distance <= size // 2, 2 * distance - 1, 2 * (size - distance)),
    )


def block_place(block, z_of, x_of):
    owner, local = block // 4, block % 4
    a = z_of(owner // (2 * NX)) % NZ
    b = x_of(owner // 2 % NX) % NX
    slot_a = a * NX + ring_pos(b, NX)
    slot_b = ring_pos(b, NX) * NZ + ring_pos(a, NZ)
    return jnp.where(local < 2, 2 * slot_a, 64 + 2 * slot_b) + local % 2, owner % 2


def kernel(
    fwd_idx, bwd_idx, rhs_hbm, inv_hbm, low_hbm, out_ref,
    rhs, inv, low, low_hi, low_lo, fwd, own_part, gath_0, gath_1, gath_2, part, col_in, rest,
    sol, terms_0, terms_1, terms_2, others_0, others_1, others_2, own, up_a, dn_a, row_x, in_x, mid_l, mid_r, fin_l, fin_r, col_z, in_z,
    load_sem, send_sem, inv_sem, ag_sem, rs_sem, col_sem,
):
    gath, terms = (gath_0, gath_1, gath_2), (terms_0, terms_1, terms_2)
    others = (others_0, others_1, others_2)
    row, c = lax.axis_index("row"), lax.axis_index("col")
    z, x, core = row // (2 * NX), row // 2 % NX, row % 2

    def at_row(zz, xx, cc):
        return ((zz * NX + xx) * 2 + cc, c)

    z_dev = [None] + [at_row((z + a) % NZ, x, core) for a in range(1, NZ)]
    x_rt, x_lf = at_row(z, (x + 1) % NX, core), at_row(z, (x + NX - 1) % NX, core)
    x_far = at_row(z, (x + 2) % NX, core)
    sib = at_row(z, x, 1 - core)
    col_dev = [None] + [(row, (c + t) % 4) for t in (1, 2, 3)]

    loads = [
        pltpu.make_async_copy(inv_hbm, inv.at[:, :, c], load_sem.at[0]),
        pltpu.make_async_copy(rhs_hbm.at[0], rhs.at[0], load_sem.at[1]),
        pltpu.make_async_copy(rhs_hbm.at[pl.ds(1, 3)], rhs.at[pl.ds(1, 3)], load_sem.at[2]),
        pltpu.make_async_copy(low_hbm, low, load_sem.at[3]),
    ]
    for load in loads:
        load.start()

    barrier = pltpu.get_barrier_semaphore()
    partners = [z_dev[a] for a in (1, 2, 6, 7)] + [x_rt, x_lf, x_far, sib] + col_dev[1:]
    for partner in partners:
        pl.semaphore_signal(barrier, inc=1, device_id=partner, device_id_type=MESH)

    for level in range(3):
        terms[level][64] = jnp.zeros((32, 128), jnp.float32)
        others[level][64] = jnp.zeros((32, 128), jnp.float32)
    loads[0].wait()
    loads[1].wait()
    for j in range(4):
        fwd[0, j] = exact_dot(inv[0, j, c], rhs[0, j])
    pl.semaphore_wait(barrier, len(partners))

    def put(src, dst, sem, device, out_sem):
        pltpu.make_async_remote_copy(
            src_ref=src, dst_ref=dst, send_sem=out_sem, recv_sem=sem, device_id=device, device_id_type=MESH
        ).start()

    def take(dst, sem, device=None):
        pltpu.make_async_remote_copy(
            src_ref=dst, dst_ref=dst, send_sem=send_sem.at[0], recv_sem=sem, device_id=sib, device_id_type=MESH
        ).wait_recv()

    def sent(count, out_sem):
        ref = gath[0].at[pl.ds(0, count)]
        pltpu.make_async_remote_copy(
            src_ref=ref, dst_ref=ref, send_sem=out_sem, recv_sem=out_sem, device_id=sib, device_id_type=MESH
        ).wait_send()

    def gather_row(level, ready, between):
        g_sem = send_sem.at[0]
        ids = {}

        def sem(key):
            return ag_sem.at[level, ids.setdefault(key, len(ids))]

        def ref_a(a, pos, count):
            return gath[level].at[pl.ds(2 * (a * NX + pos), 2 * count)]

        def ref_b(pos, zpos, count):
            return gath[level].at[pl.ds(64 + 2 * (pos * NZ + zpos), 2 * count)]

        sib_sem = sem("sib")

        def share(first, count):
            put(
                gath[level].at[pl.ds(first, count)], gath[level].at[pl.ds(128 + first, count)],
                sib_sem, sib, g_sem,
            )

        def share_a(a, pos, count):
            share(2 * (a * NX + pos), 2 * count)

        def share_b(pos, zpos, count):
            share(64 + 2 * (pos * NZ + zpos), 2 * count)

        def z_a(a, p, direction, hops=1):
            to = (a + direction * hops) % NZ
            put(ref_a(a, 2 * p, 2), ref_a(to, 2 * p, 2), sem(("az", to, p)), z_dev[direction * hops % NZ], g_sem)

        def x_b(group):
            zpos, count = GROUPS[group]
            put(ref_b(0, zpos, count), ref_b(1, zpos, count), sem(("bl", group)), x_rt, g_sem)
            put(ref_b(0, zpos, count), ref_b(2, zpos, count), sem(("br", group)), x_lf, g_sem)

        def far_b(group):
            zpos, count = GROUPS[group]
            if group in (0, 1, 4):
                put(ref_b(1, zpos, count), ref_b(3, zpos, count), sem(("b2", group)), x_rt, g_sem)
            else:
                put(ref_b(2, zpos, count), ref_b(3, zpos, count), sem(("b2", group)), x_lf, g_sem)

        def got_x_b(group):
            zpos, count = GROUPS[group]
            if group in (0, 1, 4):
                take(ref_b(1, zpos, count), sem(("bl", group)))
                far_b(group)
                take(ref_b(2, zpos, count), sem(("br", group)))
            else:
                take(ref_b(2, zpos, count), sem(("br", group)))
                far_b(group)
                take(ref_b(1, zpos, count), sem(("bl", group)))
            share_b(1, zpos, count)
            share_b(2, zpos, count)

        def got_far_b(group):
            zpos, count = GROUPS[group]
            take(ref_b(3, zpos, count), sem(("b2", group)))
            share_b(3, zpos, count)

        def z_b(a, hops):
            to = (a + hops) % NZ
            put(ref_b(0, Z_POS[a], 1), ref_b(0, Z_POS[to], 1), sem(("bz", to)), z_dev[hops % NZ], g_sem)

        def got_z_b(a):
            take(ref_b(0, Z_POS[a], 1), sem(("bz", a)))
            if a == 2:
                z_b(2, 2)
                z_b(2, 1)
            elif a == 6:
                z_b(6, -1)

        def got_z_a(a, p):
            take(ref_a(a, 2 * p, 2), sem(("az", a, p)))

        ready(level, 0)
        gath[level][pl.ds(0, 2)] = fwd[level, pl.ds(0, 2)]
        put(ref_a(0, 0, 1), ref_a(0, 1, 1), sem("ax1"), x_rt, g_sem)
        put(ref_a(0, 0, 1), ref_a(0, 3, 1), sem("ax2"), x_far, g_sem)
        put(ref_a(0, 0, 1), ref_a(0, 2, 1), sem("ax3"), x_lf, g_sem)
        share_a(0, 0, 1)
        ready(level, 1)
        gath[level][pl.ds(64, 2)] = fwd[level, pl.ds(2, 2)]
        for hops in (2, -2, 1, -1):
            z_b(0, hops)
        x_b(0)
        share_b(0, 0, 1)
        between()
        take(ref_a(0, 1, 1), sem("ax1"))
        z_a(0, 0, 1)
        z_a(0, 0, -1)
        take(ref_a(0, 2, 1), sem("ax3"))
        take(ref_a(0, 3, 1), sem("ax2"))
        z_a(0, 1, 1)
        z_a(0, 1, -1)
        share_a(0, 1, 3)
        for group, pair in ((1, (1, 7)), (2, (2, 6))):
            for a in pair:
                got_z_b(a)
            x_b(group)
            share_b(0, *GROUPS[group])
        got_x_b(0)
        for p in (0, 1):
            got_z_a(1, p)
            z_a(1, p, 1)
            got_z_a(7, p)
            z_a(7, p, -1)
        share_a(1, 0, 4)
        share_a(7, 0, 4)
        got_z_b(3)
        got_z_b(5)
        x_b(3)
        share_b(0, *GROUPS[3])
        got_x_b(1)
        got_far_b(0)
        got_z_b(4)
        x_b(4)
        share_b(0, *GROUPS[4])
        got_x_b(2)
        got_z_a(2, 0)
        z_a(2, 0, 1, 2)
        z_a(2, 0, 1)
        got_z_a(6, 0)
        z_a(6, 0, -1)
        got_z_a(6, 1)
        z_a(6, 1, -1, 2)
        z_a(6, 1, -1)
        got_z_a(2, 1)
        z_a(2, 1, 1)
        share_a(2, 0, 4)
        share_a(6, 0, 4)
        got_far_b(1)
        got_x_b(3)
        got_x_b(4)
        got_far_b(2)
        for a in (3, 5):
            got_z_a(a, 0)
            got_z_a(a, 1)
            share_a(a, 0, 4)
        got_far_b(3)
        got_far_b(4)
        got_z_a(4, 0)
        got_z_a(4, 1)
        share_a(4, 0, 4)
        take(gath[level].at[pl.ds(128, 128)], sib_sem)
        sent(252, g_sem)

    def reduce_row(low_level, build):
        r_sem = send_sem.at[0]
        ids = {}

        def sem(key):
            return rs_sem.at[low_level, ids.setdefault(key, len(ids))]

        def own_a(a, p):
            return own.at[low_level, pl.ds(2 * (a * NX + 2 * p), 4)]

        def own_b(pos, zpos, count):
            return own.at[low_level, pl.ds(64 + 2 * (pos * NZ + zpos), 2 * count)]

        def ref_az(hops, p, direction):
            return (up_a if direction == 1 else dn_a).at[low_level, hops, p]

        def send_az(src, hops, p, direction, step=1):
            slot = hops - step if step == 1 else 3
            put(src, ref_az(slot, p, direction), sem(("az", slot, p, direction)), z_dev[direction * step % NZ], r_sem)

        def pass_az(hops, p, direction):
            ref = ref_az(hops, p, direction)
            take(ref, sem(("az", hops, p, direction)))
            if hops == 2 and p == (0 if direction == 1 else 1):
                far = ref_az(3, p, direction)
                take(far, sem(("az", 3, p, direction)))
                ref[...] += own_a(direction * hops % NZ, p)[...] + far[...]
                send_az(ref, hops, p, direction)
            elif hops:
                ref[...] += own_a(direction * hops % NZ, p)[...]
                send_az(ref, hops, p, direction)

        zs = [(7, 1), (3, 4), (0, 3)]

        def mid(buffer, part_no):
            zpos, count = zs[part_no]
            return buffer.at[low_level, pl.ds(2 * zpos, 2 * count)]

        build(112, 16)
        put(own_b(3, 7, 1), mid(mid_l, 0), sem(("m", 0)), x_rt, r_sem)
        put(own_b(3, 3, 4), mid(mid_r, 1), sem(("m", 1)), x_lf, r_sem)
        put(own_b(3, 0, 3), mid(mid_l, 2), sem(("m", 2)), x_rt, r_sem)
        build(24, 24)
        send_az(own_a(4, 0), 4, 0, 1, 2)
        send_az(own_a(4, 1), 4, 1, -1, 2)
        send_az(own_a(3, 0), 3, 0, 1)
        send_az(own_a(5, 1), 3, 1, -1)
        send_az(own_a(3, 1), 3, 1, 1)
        send_az(own_a(5, 0), 3, 0, -1)
        build(80, 32)
        put(own_b(2, 7, 1), mid(fin_r, 0), sem(("fr", 0)), x_lf, r_sem)
        put(own_b(1, 3, 4), mid(fin_l, 1), sem(("fl", 1)), x_rt, r_sem)
        put(own_b(2, 0, 3), mid(fin_r, 2), sem(("fr", 2)), x_lf, r_sem)
        build(0, 24)
        build(48, 32)

        take(mid(mid_l, 0), sem(("m", 0)))
        mid(mid_l, 0)[...] += own_b(1, 7, 1)[...]
        put(mid(mid_l, 0), mid(fin_l, 0), sem(("fl", 0)), x_rt, r_sem)
        take(mid(mid_r, 1), sem(("m", 1)))
        mid(mid_r, 1)[...] += own_b(2, 3, 4)[...]
        put(mid(mid_r, 1), mid(fin_r, 1), sem(("fr", 1)), x_lf, r_sem)
        pass_az(2, 1, 1)
        pass_az(2, 0, -1)
        take(mid(mid_l, 2), sem(("m", 2)))
        mid(mid_l, 2)[...] += own_b(1, 0, 3)[...]
        put(mid(mid_l, 2), mid(fin_l, 2), sem(("fl", 2)), x_rt, r_sem)
        pass_az(2, 0, 1)
        pass_az(2, 1, -1)

        def finish_x(part_no):
            zpos, count = zs[part_no]
            take(mid(fin_l, part_no), sem(("fl", part_no)))
            take(mid(fin_r, part_no), sem(("fr", part_no)))
            col_z[low_level, pl.ds(2 * zpos, 2 * count)] = (
                own_b(0, zpos, count)[...] + mid(fin_l, part_no)[...] + mid(fin_r, part_no)[...]
            )

        def z_part(a):
            return col_z.at[low_level, pl.ds(2 * Z_POS[a], 2)]

        def send_bz(src, key, hops):
            put(src, in_z.at[low_level, key], sem(("bz", key)), z_dev[hops % NZ], r_sem)

        def got_bz(key):
            take(in_z.at[low_level, key], sem(("bz", key)))
            return in_z[low_level, key]

        finish_x(0)
        send_bz(z_part(4), 0, 2)
        pass_az(1, 1, 1)
        pass_az(1, 0, -1)
        finish_x(1)
        send_bz(z_part(3), 1, 1)
        send_bz(z_part(5), 2, -1)
        pass_az(1, 0, 1)
        pass_az(1, 1, -1)
        finish_x(2)
        send_bz(z_part(1), 5, 1)
        send_bz(z_part(7), 6, -1)
        z_part(2)[...] += got_bz(0) + got_bz(1)
        send_bz(z_part(2), 3, 2)
        z_part(6)[...] += got_bz(2)
        send_bz(z_part(6), 4, -2)
        for p in (1, 0):
            pass_az(0, p, 1)
            pass_az(0, p, -1)
            row_x[low_level, p] = own_a(0, p)[...] + up_a[low_level, 0, p] + dn_a[low_level, 0, p]
            if p == 1:
                put(row_x.at[low_level, 1, pl.ds(2, 2)], in_x.at[low_level, 2], sem("x3"), x_far, r_sem)
                put(row_x.at[low_level, 1, pl.ds(0, 2)], in_x.at[low_level, 1], sem("x2"), x_lf, r_sem)
            else:
                put(row_x.at[low_level, 0, pl.ds(2, 2)], in_x.at[low_level, 0], sem("x1"), x_rt, r_sem)
        half_b = col_z[low_level, pl.ds(0, 2)]
        for key in (5, 6, 3, 4):
            half_b = half_b + got_bz(key)
        start_solve(low_level, 1, fwd[low_level, pl.ds(2, 2)] - half_b)
        for slot in (2, 1, 0):
            take(in_x.at[low_level, slot], sem("x%d" % (slot + 1)))
        half_a = (
            row_x[low_level, 0, pl.ds(0, 2)] + in_x[low_level, 0] + in_x[low_level, 1] + in_x[low_level, 2]
        )
        start_solve(low_level, 0, fwd[low_level, pl.ds(0, 2)] - half_a)
        sent(188, r_sem)

    for level in (1, 2, 3, 0):
        for t in (1, 2, 3):
            ref = inv.at[level, :, c]
            put(ref, ref, inv_sem.at[level, t - 1], col_dev[t], send_sem.at[1])

    def whole_inv(level):
        for t in (1, 2, 3):
            take(inv.at[level, :, 0], inv_sem.at[level, t - 1])

    def forward_level(low_level):
        level = low_level + 1

        def between():
            if low_level == 0:
                loads[2].wait()
                loads[3].wait()

            for j in range(4):
                own_part[j] = exact_dot(inv[level, j, c], rhs[level, j])
            for j in range(4):
                low_hi[j], low_lo[j] = split(low[low_level, j].T)

        gather_row(low_level, finish_forward, between)
        whole_inv(level)
        for half in (0, 1):
            for j in (2 * half, 2 * half + 1):
                picked = jnp.concatenate(
                    [gath[low_level][fwd_idx[low_level, 16 * j + d]] for d in range(16)], axis=0
                )
                update = split_dot((low_hi[j], low_lo[j]), split(picked))
                done = exact_dot(inv[level, j].reshape(128, 128), update)
                for piece in range(4):
                    part[low_level, piece, j] = done[32 * piece : 32 * piece + 32]
            for t in (2, 1, 3):
                put(
                    part.at[low_level, (c + t) % 4, pl.ds(2 * half, 2)],
                    col_in.at[low_level, t - 1, pl.ds(2 * half, 2)],
                    col_sem.at[low_level, half, t - 1], col_dev[t], send_sem.at[2],
                )

    def finish_forward(level, half):
        if level == 0:
            return
        blocks = pl.ds(2 * half, 2)
        total = own_part[blocks] - part[level - 1, c, blocks]
        for t in (1, 3, 2):
            take(col_in.at[level - 1, t - 1, blocks], col_sem.at[level - 1, half, t - 1])
            total = total - col_in[level - 1, t - 1, blocks]
        fwd[level, blocks] = total

    for low_level in range(3):
        forward_level(low_level)
    whole_inv(0)

    def start_solve(level, half, value):
        blocks = pl.ds(2 * half, 2)
        rest[level, c, blocks] = value
        ref = rest.at[level, c, blocks]
        for t in (2, 1, 3):
            put(ref, ref, col_sem.at[3 + level, half, t - 1], col_dev[t], send_sem.at[2])

    def finish_solve(level, half, product):
        blocks = pl.ds(2 * half, 2)
        for t in (1, 3, 2):
            take(rest.at[level, c, blocks], col_sem.at[3 + level, half, t - 1])
        for j in (2 * half, 2 * half + 1):
            whole = inv[level, j].reshape(128, 128)
            sol[j] = exact_dot(whole.T, rest[level, :, j].reshape(128, 128))
            product(j)
            out_ref[level, j] = sol[j, pl.ds(pl.multiple_of(32 * c, 32), 32), :]

    for half in (1, 0):
        finish_forward(3, half)
        start_solve(3, half, fwd[3, pl.ds(2 * half, 2)])

    def backward_level(low_level):
        t_sem = rs_sem.at[low_level, 63]

        def product(j):
            value = exact_dot(low[low_level, j], sol[j])
            terms[low_level][pl.ds(16 * j, 16)] = value.reshape(16, 32, 128)
            put(
                terms[low_level].at[pl.ds(16 * j, 16)], others[low_level].at[pl.ds(16 * j, 16)],
                t_sem, sib, send_sem.at[0],
            )

        finish_solve(low_level + 1, 1, product)
        finish_solve(low_level + 1, 0, product)

        def build_mine(place, inner):
            own[low_level, place] = (
                terms[low_level][bwd_idx[low_level, 4 * place]]
                + terms[low_level][bwd_idx[low_level, 4 * place + 1]]
            )
            return inner

        def build_other(place, inner):
            own[low_level, place] += (
                others[low_level][bwd_idx[low_level, 4 * place + 2]]
                + others[low_level][bwd_idx[low_level, 4 * place + 3]]
            )
            return inner

        lax.fori_loop(0, 128, build_mine, 0, unroll=8)
        take(others[low_level].at[pl.ds(0, 64)], t_sem)

        def build(first, count):
            lax.fori_loop(first, first + count, build_other, 0, unroll=8)

        reduce_row(low_level, build)

    for low_level in (2, 1, 0):
        backward_level(low_level)
    for half in (1, 0):
        finish_solve(0, half, lambda j: None)
    sent(48, send_sem.at[1])
    sent(84, send_sem.at[2])


def on_device(right_sides, inverse_diag, lower_blocks, depends_on):
    row = lax.axis_index("row")
    z, x, core = row // (2 * NX), row // 2 % NX, row % 2
    mine = lax.dynamic_slice(depends_on, (0, 4 * row, 0), (3, 4, 16)).reshape(3, 64)
    other = lax.dynamic_slice(depends_on, (0, 4 * (row + 1 - 2 * core), 0), (3, 4, 16)).reshape(3, 64)
    place, owner_core = block_place(mine, lambda zz: z - zz, lambda xx: x - xx)
    fwd_idx = place + jnp.where(owner_core == core, 0, 128)
    lists = []
    for wanted in (mine, other):
        place, owner_core = block_place(wanted, lambda zz: zz - z, lambda xx: xx - x)
        place = jnp.where(owner_core == core, place, -1)
        match = place[:, None, :] == jnp.arange(128, dtype=jnp.int32)[None, :, None]
        entry = jnp.arange(64, dtype=jnp.int32)[None, None, :]
        first = jnp.min(jnp.where(match, entry, 64), axis=2)
        last = jnp.max(jnp.where(match, entry, -1), axis=2)
        lists.append(first)
        lists.append(jnp.where(last > first, last, 64))
    bwd_idx = jnp.stack(lists, axis=2).reshape(3, 512)

    f32 = jnp.float32

    def vmem(*shape):
        return pltpu.VMEM(shape, f32)

    any_spec = pl.BlockSpec(memory_space=pl.ANY)
    smem_spec = pl.BlockSpec(memory_space=pltpu.SMEM)
    block = (32, 128)
    return pl.pallas_call(
        kernel,
        out_shape=jax.ShapeDtypeStruct((4, 4, 32, 128), f32),
        in_specs=[smem_spec, smem_spec, any_spec, any_spec, any_spec],
        out_specs=pl.BlockSpec(memory_space=pltpu.VMEM),
        scratch_shapes=[
            vmem(4, 4, 128, 128),
            vmem(4, 4, 4, *block),
            vmem(3, 4, 512, 128),
            pltpu.VMEM((4, 128, 512), jnp.bfloat16),
            pltpu.VMEM((4, 128, 512), jnp.bfloat16),
            vmem(4, 4, *block),
            vmem(4, *block),
            vmem(256, *block),
            vmem(256, *block),
            vmem(256, *block),
            vmem(3, 4, 4, *block),
            vmem(3, 3, 4, *block),
            vmem(4, 4, 4, *block),
            vmem(4, 128, 128),
            vmem(65, *block),
            vmem(65, *block),
            vmem(65, *block),
            vmem(65, *block),
            vmem(65, *block),
            vmem(65, *block),
            vmem(3, 128, *block),
            vmem(3, 4, 2, 4, *block),
            vmem(3, 4, 2, 4, *block),
            vmem(3, 2, 4, *block),
            vmem(3, 3, 2, *block),
            vmem(3, 16, *block),
            vmem(3, 16, *block),
            vmem(3, 16, *block),
            vmem(3, 16, *block),
            vmem(3, 16, *block),
            vmem(3, 7, 2, *block),
            pltpu.SemaphoreType.DMA((4,)),
            pltpu.SemaphoreType.DMA((3,)),
            pltpu.SemaphoreType.DMA((4, 3)),
            pltpu.SemaphoreType.DMA((3, 64)),
            pltpu.SemaphoreType.DMA((3, 64)),
            pltpu.SemaphoreType.DMA((7, 2, 3)),
        ],
        compiler_params=pltpu.CompilerParams(
            collective_id=0, has_side_effects=True, vmem_limit_bytes=60 * 1024 * 1024
        ),
    )(fwd_idx, bwd_idx, right_sides, inverse_diag, lower_blocks.reshape(3, 4, 512, 128))


def solution(mesh):
    return jax.shard_map(
        on_device,
        mesh=mesh,
        in_specs=(
            P(None, "row", None, None),
            P(None, "row", "col", None),
            P(None, "row", None, "col", None),
            P(),
        ),
        out_specs=P(None, "row", "col", None),
        check_vma=False,
    )
```

```python
import jax
import jax.numpy as jnp
from jax import lax
from jax.experimental import pallas as pl
from jax.experimental.pallas import tpu as pltpu
from jax.sharding import PartitionSpec as P

MESH = pl.DeviceIdType.MESH
NZ, NX = 8, 4
Z_POS = {0: 0, 1: 1, 7: 2, 2: 3, 6: 4, 3: 5, 5: 6, 4: 7}
ROUTES = (
    (0, 0, 1, 0, 1, 1, ()),
    (0, 0, -1, 0, 2, 1, ()),
    (0, 1, 0, 0, 4, 1, ()),
    (0, -1, 0, 0, 28, 1, ()),
    (0, 0, 2, 0, 3, 1, ()),
    (1, 1, 0, 0, 1, 1, ()),
    (1, -1, 0, 0, 2, 1, ()),
    (1, 0, -1, 0, 16, 1, ()),
    (1, 0, 1, 0, 8, 1, ()),
    (1, 3, 0, 0, 5, 1, ()),
    (1, -3, 0, 0, 6, 1, ()),
    (0, 1, 0, 1, 5, 1, (0,)),
    (0, -1, 0, 1, 29, 1, (0,)),
    (0, 1, 0, 2, 6, 1, (1,)),
    (0, -1, 0, 2, 30, 1, (1,)),
    (0, 1, 0, 4, 8, 1, (2,)),
    (0, -1, 0, 28, 24, 1, (3,)),
    (1, 0, 1, 1, 9, 2, (5, 6)),
    (1, 0, -1, 1, 17, 2, (5, 6)),
    (0, 1, 0, 3, 7, 1, (4,)),
    (0, -1, 0, 3, 31, 1, (4,)),
    (1, 0, 1, 8, 24, 1, (8,)),
    (1, 1, 0, 1, 3, 1, (5,)),
    (1, -1, 0, 2, 4, 1, (6,)),
    (1, 1, 0, 5, 7, 1, (9,)),
    (0, -1, 0, 29, 25, 1, (12,)),
    (1, 0, 1, 5, 13, 2, (9, 10)),
    (1, 0, -1, 5, 21, 2, (9, 10)),
    (0, 1, 0, 5, 9, 1, (11,)),
    (0, -1, 0, 30, 26, 1, (14,)),
    (0, 1, 0, 6, 10, 1, (13,)),
    (0, -1, 0, 24, 20, 1, (16,)),
    (0, 1, 0, 8, 12, 1, (15,)),
    (0, -1, 0, 31, 27, 1, (20,)),
    (1, 0, -1, 17, 25, 2, (18,)),
    (0, 2, 0, 8, 16, 1, (15,)),
    (1, 0, 1, 3, 11, 2, (22, 23)),
    (1, 0, -1, 3, 19, 2, (22, 23)),
    (0, -1, 0, 25, 21, 1, (25,)),
    (0, 1, 0, 7, 11, 1, (19,)),
    (1, 0, 1, 7, 15, 1, (24,)),
    (1, 0, -1, 7, 23, 1, (24,)),
    (0, -1, 0, 26, 22, 1, (29,)),
    (0, 1, 0, 9, 13, 1, (28,)),
    (1, 0, -1, 21, 29, 2, (27,)),
    (0, -2, 0, 26, 18, 1, (29,)),
    (0, 2, 0, 9, 17, 1, (28,)),
    (0, -1, 0, 27, 23, 1, (33,)),
    (0, 1, 0, 10, 14, 1, (30,)),
    (0, 1, 0, 11, 15, 1, (39,)),
    (1, 0, 1, 11, 27, 2, (36,)),
    (0, -2, 0, 27, 19, 1, (33,)),
    (1, 0, 1, 15, 31, 1, (40,)),
)


def split(v):
    high = v.astype(jnp.bfloat16)
    return high, (v - high.astype(jnp.float32)).astype(jnp.bfloat16)


def split_dot(a, b):
    def dot(u, v):
        return jnp.dot(u, v, preferred_element_type=jnp.float32)

    return dot(a[0], b[0]) + (dot(a[0], b[1]) + dot(a[1], b[0]))


def exact_dot(a, b):
    return split_dot(split(a), split(b))


def ring_pos(distance, size):
    return jnp.where(
        distance == 0,
        0,
        jnp.where(distance <= size // 2, 2 * distance - 1, 2 * (size - distance)),
    )


def block_place(block, z_of, x_of):
    owner, local = block // 4, block % 4
    a = z_of(owner // (2 * NX)) % NZ
    b = x_of(owner // 2 % NX) % NX
    slot_a = a * NX + ring_pos(b, NX)
    slot_b = ring_pos(b, NX) * NZ + ring_pos(a, NZ)
    return jnp.where(local < 2, 2 * slot_a, 64 + 2 * slot_b) + local % 2, owner % 2


def kernel(
    fwd_idx, bwd_idx, rhs_hbm, inv_hbm, low_hbm, out_ref,
    rhs, inv, low, low_hi, low_lo, fwd, own_part, gath_0, gath_1, gath_2, part, col_in, rest,
    sol, terms_0, terms_1, terms_2, others_0, others_1, others_2, own, up_a, dn_a, row_x, in_x, mid_l, mid_r, fin_l, fin_r, col_z, in_z,
    load_sem, send_sem, inv_sem, ag_sem, rs_sem, col_sem,
):
    gath, terms = (gath_0, gath_1, gath_2), (terms_0, terms_1, terms_2)
    others = (others_0, others_1, others_2)
    row, c = lax.axis_index("row"), lax.axis_index("col")
    z, x, core = row // (2 * NX), row // 2 % NX, row % 2

    def at_row(zz, xx, cc):
        return ((zz * NX + xx) * 2 + cc, c)

    z_dev = [None] + [at_row((z + a) % NZ, x, core) for a in range(1, NZ)]
    x_rt, x_lf = at_row(z, (x + 1) % NX, core), at_row(z, (x + NX - 1) % NX, core)
    x_far = at_row(z, (x + 2) % NX, core)
    x_dev = [None, x_rt, x_far, x_lf]
    sib = at_row(z, x, 1 - core)
    col_dev = [None] + [(row, (c + t) % 4) for t in (1, 2, 3)]

    loads = [
        pltpu.make_async_copy(inv_hbm, inv.at[:, :, c], load_sem.at[0]),
        pltpu.make_async_copy(rhs_hbm.at[0], rhs.at[0], load_sem.at[1]),
        pltpu.make_async_copy(rhs_hbm.at[pl.ds(1, 3)], rhs.at[pl.ds(1, 3)], load_sem.at[2]),
        pltpu.make_async_copy(low_hbm, low, load_sem.at[3]),
    ]
    for load in loads:
        load.start()

    barrier = pltpu.get_barrier_semaphore()
    partners = [z_dev[a] for a in (1, 2, 3, 5, 6, 7)] + x_dev[1:] + [sib] + col_dev[1:]
    for partner in partners:
        pl.semaphore_signal(barrier, inc=1, device_id=partner, device_id_type=MESH)

    for level in range(3):
        terms[level][64] = jnp.zeros((32, 128), jnp.float32)
        others[level][64] = jnp.zeros((32, 128), jnp.float32)
    loads[0].wait()
    loads[1].wait()
    for j in range(4):
        fwd[0, j] = exact_dot(inv[0, j, c], rhs[0, j])
    pl.semaphore_wait(barrier, len(partners))

    def put(src, dst, sem, device, out_sem):
        pltpu.make_async_remote_copy(
            src_ref=src, dst_ref=dst, send_sem=out_sem, recv_sem=sem, device_id=device, device_id_type=MESH
        ).start()

    def take(dst, sem, device=None):
        pltpu.make_async_remote_copy(
            src_ref=dst, dst_ref=dst, send_sem=send_sem.at[0], recv_sem=sem, device_id=sib, device_id_type=MESH
        ).wait_recv()

    def sent(count, out_sem):
        ref = gath[0].at[pl.ds(0, count)]
        pltpu.make_async_remote_copy(
            src_ref=ref, dst_ref=ref, send_sem=out_sem, recv_sem=out_sem, device_id=sib, device_id_type=MESH
        ).wait_send()

    def gather_row(level, ready, between):
        g_sem = send_sem.at[0]
        sib_sem = ag_sem.at[level, 95]
        issued = set()

        def ref(half, slot, count, plane=0):
            return gath[level].at[pl.ds(128 * plane + 64 * half + 2 * slot, 2 * count)]

        def share(half, slot, count):
            put(ref(half, slot, count), ref(half, slot, count, 1), sib_sem, sib, g_sem)

        def issue(arrived, halves):
            for number, (half, dz, dx, src, dst, count, needs) in enumerate(ROUTES):
                if number in issued or half not in halves or any(need >= arrived for need in needs):
                    continue
                issued.add(number)
                device = z_dev[dz % NZ] if dz else x_dev[dx % NX]
                put(ref(half, src, count), ref(half, dst, count), ag_sem.at[level, number], device, g_sem)

        for half in (0, 1):
            ready(level, half)
            gath[level][pl.ds(64 * half, 2)] = fwd[level, pl.ds(2 * half, 2)]
            issue(0, range(half + 1))
            share(half, 0, 1)
        between()
        for number, (half, dz, dx, src, dst, count, needs) in enumerate(ROUTES):
            take(ref(half, dst, count), ag_sem.at[level, number])
            issue(number + 1, (0, 1))
            share(half, dst, count)
        take(gath[level].at[pl.ds(128, 128)], sib_sem)
        sent(2 * sum(route[5] for route in ROUTES) + 128, g_sem)

    def reduce_row(low_level, build):
        r_sem = send_sem.at[0]
        ids = {}

        def sem(key):
            return rs_sem.at[low_level, ids.setdefault(key, len(ids))]

        def own_a(a, p):
            return own.at[low_level, pl.ds(2 * (a * NX + 2 * p), 4)]

        def own_b(pos, zpos, count):
            return own.at[low_level, pl.ds(64 + 2 * (pos * NZ + zpos), 2 * count)]

        def ref_az(hops, p, direction):
            return (up_a if direction == 1 else dn_a).at[low_level, hops, p]

        def send_az(src, hops, p, direction, step=1):
            slot = hops - step if step == 1 else 3
            put(src, ref_az(slot, p, direction), sem(("az", slot, p, direction)), z_dev[direction * step % NZ], r_sem)

        def pass_az(hops, p, direction):
            ref = ref_az(hops, p, direction)
            take(ref, sem(("az", hops, p, direction)))
            if hops == 2 and p == (0 if direction == 1 else 1):
                far = ref_az(3, p, direction)
                take(far, sem(("az", 3, p, direction)))
                ref[...] += own_a(direction * hops % NZ, p)[...] + far[...]
                send_az(ref, hops, p, direction)
            elif hops:
                ref[...] += own_a(direction * hops % NZ, p)[...]
                send_az(ref, hops, p, direction)

        zs = [(7, 1), (3, 4), (0, 3)]

        def mid(buffer, part_no):
            zpos, count = zs[part_no]
            return buffer.at[low_level, pl.ds(2 * zpos, 2 * count)]

        build(112, 16)
        put(own_b(3, 7, 1), mid(mid_l, 0), sem(("m", 0)), x_rt, r_sem)
        put(own_b(3, 3, 4), mid(mid_r, 1), sem(("m", 1)), x_lf, r_sem)
        put(own_b(3, 0, 3), mid(mid_l, 2), sem(("m", 2)), x_rt, r_sem)
        build(24, 24)
        send_az(own_a(4, 0), 4, 0, 1, 2)
        send_az(own_a(4, 1), 4, 1, -1, 2)
        send_az(own_a(3, 0), 3, 0, 1)
        send_az(own_a(5, 1), 3, 1, -1)
        send_az(own_a(3, 1), 3, 1, 1)
        send_az(own_a(5, 0), 3, 0, -1)
        build(80, 32)
        put(own_b(2, 7, 1), mid(fin_r, 0), sem(("fr", 0)), x_lf, r_sem)
        put(own_b(1, 3, 4), mid(fin_l, 1), sem(("fl", 1)), x_rt, r_sem)
        put(own_b(2, 0, 3), mid(fin_r, 2), sem(("fr", 2)), x_lf, r_sem)
        build(0, 24)
        build(48, 32)

        take(mid(mid_l, 0), sem(("m", 0)))
        mid(mid_l, 0)[...] += own_b(1, 7, 1)[...]
        put(mid(mid_l, 0), mid(fin_l, 0), sem(("fl", 0)), x_rt, r_sem)
        take(mid(mid_r, 1), sem(("m", 1)))
        mid(mid_r, 1)[...] += own_b(2, 3, 4)[...]
        put(mid(mid_r, 1), mid(fin_r, 1), sem(("fr", 1)), x_lf, r_sem)
        pass_az(2, 1, 1)
        pass_az(2, 0, -1)
        take(mid(mid_l, 2), sem(("m", 2)))
        mid(mid_l, 2)[...] += own_b(1, 0, 3)[...]
        put(mid(mid_l, 2), mid(fin_l, 2), sem(("fl", 2)), x_rt, r_sem)
        pass_az(2, 0, 1)
        pass_az(2, 1, -1)

        def finish_x(part_no):
            zpos, count = zs[part_no]
            take(mid(fin_l, part_no), sem(("fl", part_no)))
            take(mid(fin_r, part_no), sem(("fr", part_no)))
            col_z[low_level, pl.ds(2 * zpos, 2 * count)] = (
                own_b(0, zpos, count)[...] + mid(fin_l, part_no)[...] + mid(fin_r, part_no)[...]
            )

        def z_part(a):
            return col_z.at[low_level, pl.ds(2 * Z_POS[a], 2)]

        def send_bz(src, key, hops):
            put(src, in_z.at[low_level, key], sem(("bz", key)), z_dev[hops % NZ], r_sem)

        def got_bz(key):
            take(in_z.at[low_level, key], sem(("bz", key)))
            return in_z[low_level, key]

        finish_x(0)
        send_bz(z_part(4), 0, 2)
        pass_az(1, 1, 1)
        pass_az(1, 0, -1)
        finish_x(1)
        send_bz(z_part(3), 1, 1)
        send_bz(z_part(5), 2, -1)
        pass_az(1, 0, 1)
        pass_az(1, 1, -1)
        finish_x(2)
        send_bz(z_part(1), 5, 1)
        send_bz(z_part(7), 6, -1)
        z_part(2)[...] += got_bz(0) + got_bz(1)
        send_bz(z_part(2), 3, 2)
        z_part(6)[...] += got_bz(2)
        send_bz(z_part(6), 4, -2)
        for p in (1, 0):
            pass_az(0, p, 1)
            pass_az(0, p, -1)
            row_x[low_level, p] = own_a(0, p)[...] + up_a[low_level, 0, p] + dn_a[low_level, 0, p]
            if p == 1:
                put(row_x.at[low_level, 1, pl.ds(2, 2)], in_x.at[low_level, 2], sem("x3"), x_far, r_sem)
                put(row_x.at[low_level, 1, pl.ds(0, 2)], in_x.at[low_level, 1], sem("x2"), x_lf, r_sem)
            else:
                put(row_x.at[low_level, 0, pl.ds(2, 2)], in_x.at[low_level, 0], sem("x1"), x_rt, r_sem)
        half_b = col_z[low_level, pl.ds(0, 2)]
        for key in (5, 6, 3, 4):
            half_b = half_b + got_bz(key)
        start_solve(low_level, 1, fwd[low_level, pl.ds(2, 2)] - half_b)
        for slot in (2, 1, 0):
            take(in_x.at[low_level, slot], sem("x%d" % (slot + 1)))
        half_a = (
            row_x[low_level, 0, pl.ds(0, 2)] + in_x[low_level, 0] + in_x[low_level, 1] + in_x[low_level, 2]
        )
        start_solve(low_level, 0, fwd[low_level, pl.ds(0, 2)] - half_a)
        sent(188, r_sem)

    for level in (1, 2, 3, 0):
        for t in (1, 2, 3):
            ref = inv.at[level, :, c]
            put(ref, ref, inv_sem.at[level, t - 1], col_dev[t], send_sem.at[1])

    def whole_inv(level):
        for t in (1, 2, 3):
            take(inv.at[level, :, 0], inv_sem.at[level, t - 1])

    def forward_level(low_level):
        level = low_level + 1

        def between():
            if low_level == 0:
                loads[2].wait()
                loads[3].wait()

            for j in range(4):
                own_part[j] = exact_dot(inv[level, j, c], rhs[level, j])
            for j in range(4):
                low_hi[j], low_lo[j] = split(low[low_level, j].T)

        gather_row(low_level, finish_forward, between)
        whole_inv(level)
        for half in (0, 1):
            for j in (2 * half, 2 * half + 1):
                picked = jnp.concatenate(
                    [gath[low_level][fwd_idx[low_level, 4 * core + j, d]] for d in range(16)], axis=0
                )
                update = split_dot((low_hi[j], low_lo[j]), split(picked))
                done = exact_dot(inv[level, j].reshape(128, 128), update)
                for piece in range(4):
                    part[low_level, piece, j] = done[32 * piece : 32 * piece + 32]
            for t in (2, 1, 3):
                put(
                    part.at[low_level, (c + t) % 4, pl.ds(2 * half, 2)],
                    col_in.at[low_level, t - 1, pl.ds(2 * half, 2)],
                    col_sem.at[low_level, half, t - 1], col_dev[t], send_sem.at[2],
                )

    def finish_forward(level, half):
        if level == 0:
            return
        blocks = pl.ds(2 * half, 2)
        total = own_part[blocks] - part[level - 1, c, blocks]
        for t in (1, 3, 2):
            take(col_in.at[level - 1, t - 1, blocks], col_sem.at[level - 1, half, t - 1])
            total = total - col_in[level - 1, t - 1, blocks]
        fwd[level, blocks] = total

    for low_level in range(3):
        forward_level(low_level)
    whole_inv(0)

    def start_solve(level, half, value):
        blocks = pl.ds(2 * half, 2)
        rest[level, c, blocks] = value
        ref = rest.at[level, c, blocks]
        for t in (2, 1, 3):
            put(ref, ref, col_sem.at[3 + level, half, t - 1], col_dev[t], send_sem.at[2])

    def finish_solve(level, half, product):
        blocks = pl.ds(2 * half, 2)
        for t in (1, 3, 2):
            take(rest.at[level, c, blocks], col_sem.at[3 + level, half, t - 1])
        for j in (2 * half, 2 * half + 1):
            whole = inv[level, j].reshape(128, 128)
            sol[j] = exact_dot(whole.T, rest[level, :, j].reshape(128, 128))
            product(j)
            out_ref[level, j] = sol[j, pl.ds(pl.multiple_of(32 * c, 32), 32), :]

    for half in (1, 0):
        finish_forward(3, half)
        start_solve(3, half, fwd[3, pl.ds(2 * half, 2)])

    def backward_level(low_level):
        t_sem = rs_sem.at[low_level, 63]

        def product(j):
            value = exact_dot(low[low_level, j], sol[j])
            terms[low_level][pl.ds(16 * j, 16)] = value.reshape(16, 32, 128)
            put(
                terms[low_level].at[pl.ds(16 * j, 16)], others[low_level].at[pl.ds(16 * j, 16)],
                t_sem, sib, send_sem.at[0],
            )

        finish_solve(low_level + 1, 1, product)
        finish_solve(low_level + 1, 0, product)

        def build_mine(place, inner):
            own[low_level, place] = (
                terms[low_level][bwd_idx[low_level, place]]
                + terms[low_level][bwd_idx[low_level, 128 + place]]
            )
            return inner

        def build_other(place, inner):
            own[low_level, place] += (
                others[low_level][bwd_idx[low_level, 256 + place]]
                + others[low_level][bwd_idx[low_level, 384 + place]]
            )
            return inner

        lax.fori_loop(0, 128, build_mine, 0, unroll=8)
        take(others[low_level].at[pl.ds(0, 64)], t_sem)

        def build(first, count):
            lax.fori_loop(first, first + count, build_other, 0, unroll=8)

        reduce_row(low_level, build)

    for low_level in (2, 1, 0):
        backward_level(low_level)
    for half in (1, 0):
        finish_solve(0, half, lambda j: None)
    sent(48, send_sem.at[1])
    sent(84, send_sem.at[2])


def on_device(right_sides, inverse_diag, lower_blocks, depends_on):
    row = lax.axis_index("row")
    z, x, core = row // (2 * NX), row // 2 % NX, row % 2
    wanted = lax.dynamic_slice(depends_on, (0, 4 * (row - core), 0), (3, 8, 16))
    place, owner_core = block_place(wanted, lambda zz: z - zz, lambda xx: x - xx)
    fwd_idx = place + jnp.where(owner_core == core, 0, 128)
    place, owner_core = block_place(wanted, lambda zz: zz - z, lambda xx: xx - x)
    place = jnp.where(owner_core == core, place, -1)
    match = place[:, :, :, None] == jnp.arange(128, dtype=jnp.int32)
    entry = 16 * (jnp.arange(8, dtype=jnp.int32) % 4)[:, None] + jnp.arange(16, dtype=jnp.int32)
    owner = (jnp.arange(8, dtype=jnp.int32) // 4)[:, None]
    lists = []
    for source in (core, 1 - core):
        found = match & (owner == source)[:, :, None]
        first = jnp.min(jnp.where(found, entry[:, :, None], 64), axis=(1, 2))
        last = jnp.max(jnp.where(found, entry[:, :, None], -1), axis=(1, 2))
        lists.append(first)
        lists.append(jnp.where(last > first, last, 64))
    bwd_idx = jnp.concatenate(lists, axis=1)

    f32 = jnp.float32

    def vmem(*shape):
        return pltpu.VMEM(shape, f32)

    any_spec = pl.BlockSpec(memory_space=pl.ANY)
    smem_spec = pl.BlockSpec(memory_space=pltpu.SMEM)
    block = (32, 128)
    return pl.pallas_call(
        kernel,
        out_shape=jax.ShapeDtypeStruct((4, 4, 32, 128), f32),
        in_specs=[smem_spec, smem_spec, any_spec, any_spec, any_spec],
        out_specs=pl.BlockSpec(memory_space=pltpu.VMEM),
        scratch_shapes=[
            vmem(4, 4, 128, 128),
            vmem(4, 4, 4, *block),
            vmem(3, 4, 512, 128),
            pltpu.VMEM((4, 128, 512), jnp.bfloat16),
            pltpu.VMEM((4, 128, 512), jnp.bfloat16),
            vmem(4, 4, *block),
            vmem(4, *block),
            vmem(256, *block),
            vmem(256, *block),
            vmem(256, *block),
            vmem(3, 4, 4, *block),
            vmem(3, 3, 4, *block),
            vmem(4, 4, 4, *block),
            vmem(4, 128, 128),
            vmem(65, *block),
            vmem(65, *block),
            vmem(65, *block),
            vmem(65, *block),
            vmem(65, *block),
            vmem(65, *block),
            vmem(3, 128, *block),
            vmem(3, 4, 2, 4, *block),
            vmem(3, 4, 2, 4, *block),
            vmem(3, 2, 4, *block),
            vmem(3, 3, 2, *block),
            vmem(3, 16, *block),
            vmem(3, 16, *block),
            vmem(3, 16, *block),
            vmem(3, 16, *block),
            vmem(3, 16, *block),
            vmem(3, 7, 2, *block),
            pltpu.SemaphoreType.DMA((4,)),
            pltpu.SemaphoreType.DMA((3,)),
            pltpu.SemaphoreType.DMA((4, 3)),
            pltpu.SemaphoreType.DMA((3, 96)),
            pltpu.SemaphoreType.DMA((3, 64)),
            pltpu.SemaphoreType.DMA((7, 2, 3)),
        ],
        compiler_params=pltpu.CompilerParams(
            collective_id=0, has_side_effects=True, vmem_limit_bytes=60 * 1024 * 1024
        ),
    )(fwd_idx, bwd_idx, right_sides, inverse_diag, lower_blocks.reshape(3, 4, 512, 128))


def solution(mesh):
    return jax.shard_map(
        on_device,
        mesh=mesh,
        in_specs=(
            P(None, "row", None, None),
            P(None, "row", "col", None),
            P(None, "row", None, "col", None),
            P(),
        ),
        out_specs=P(None, "row", "col", None),
        check_vma=False,
    )
```

```python
import jax
import jax.numpy as jnp
from jax import lax
from jax.experimental import pallas as pl
from jax.experimental.pallas import tpu as pltpu
from jax.sharding import PartitionSpec as P

MESH = pl.DeviceIdType.MESH
NZ, NX = 8, 4
Z_POS = {0: 0, 1: 1, 7: 2, 2: 3, 6: 4, 3: 5, 5: 6, 4: 7}
ROUTES = (
    (0, 0, 1, 0, 1, 1, ()),
    (0, 0, -1, 0, 2, 1, ()),
    (0, 1, 0, 0, 4, 1, ()),
    (0, -1, 0, 0, 28, 1, ()),
    (0, 0, 2, 0, 3, 1, ()),
    (1, 1, 0, 0, 1, 1, ()),
    (1, -1, 0, 0, 2, 1, ()),
    (1, 0, -1, 0, 16, 1, ()),
    (1, 0, 1, 0, 8, 1, ()),
    (1, 3, 0, 0, 5, 1, ()),
    (1, -3, 0, 0, 6, 1, ()),
    (0, 1, 0, 1, 5, 1, (0,)),
    (0, -1, 0, 1, 29, 1, (0,)),
    (0, 1, 0, 2, 6, 1, (1,)),
    (0, -1, 0, 2, 30, 1, (1,)),
    (0, 1, 0, 4, 8, 1, (2,)),
    (0, -1, 0, 28, 24, 1, (3,)),
    (1, 0, 1, 1, 9, 2, (5, 6)),
    (1, 0, -1, 1, 17, 2, (5, 6)),
    (0, 1, 0, 3, 7, 1, (4,)),
    (0, -1, 0, 3, 31, 1, (4,)),
    (1, 0, 1, 8, 24, 1, (8,)),
    (1, 1, 0, 1, 3, 1, (5,)),
    (1, -1, 0, 2, 4, 1, (6,)),
    (1, 1, 0, 5, 7, 1, (9,)),
    (0, -1, 0, 29, 25, 1, (12,)),
    (1, 0, 1, 5, 13, 2, (9, 10)),
    (1, 0, -1, 5, 21, 2, (9, 10)),
    (0, 1, 0, 5, 9, 1, (11,)),
    (0, -1, 0, 30, 26, 1, (14,)),
    (0, 1, 0, 6, 10, 1, (13,)),
    (0, -1, 0, 24, 20, 1, (16,)),
    (0, 1, 0, 8, 12, 1, (15,)),
    (0, -1, 0, 31, 27, 1, (20,)),
    (1, 0, -1, 17, 25, 2, (18,)),
    (0, 2, 0, 8, 16, 1, (15,)),
    (1, 0, 1, 3, 11, 2, (22, 23)),
    (1, 0, -1, 3, 19, 2, (22, 23)),
    (0, -1, 0, 25, 21, 1, (25,)),
    (0, 1, 0, 7, 11, 1, (19,)),
    (1, 0, 1, 7, 15, 1, (24,)),
    (1, 0, -1, 7, 23, 1, (24,)),
    (0, -1, 0, 26, 22, 1, (29,)),
    (0, 1, 0, 9, 13, 1, (28,)),
    (1, 0, -1, 21, 29, 2, (27,)),
    (0, -2, 0, 26, 18, 1, (29,)),
    (0, 2, 0, 9, 17, 1, (28,)),
    (0, -1, 0, 27, 23, 1, (33,)),
    (0, 1, 0, 10, 14, 1, (30,)),
    (0, 1, 0, 11, 15, 1, (39,)),
    (1, 0, 1, 11, 27, 2, (36,)),
    (0, -2, 0, 27, 19, 1, (33,)),
    (1, 0, 1, 15, 31, 1, (40,)),
)


def split(v):
    high = v.astype(jnp.bfloat16)
    return high, (v - high.astype(jnp.float32)).astype(jnp.bfloat16)


def split_dot(a, b):
    def dot(u, v):
        return jnp.dot(u, v, preferred_element_type=jnp.float32)

    return dot(a[0], b[0]) + (dot(a[0], b[1]) + dot(a[1], b[0]))


def exact_dot(a, b):
    return split_dot(split(a), split(b))


def ring_pos(distance, size):
    return jnp.where(
        distance == 0,
        0,
        jnp.where(distance <= size // 2, 2 * distance - 1, 2 * (size - distance)),
    )


def block_place(block, z_of, x_of):
    owner, local = block // 4, block % 4
    a = z_of(owner // (2 * NX)) % NZ
    b = x_of(owner // 2 % NX) % NX
    slot_a = a * NX + ring_pos(b, NX)
    slot_b = ring_pos(b, NX) * NZ + ring_pos(a, NZ)
    return jnp.where(local < 2, 2 * slot_a, 64 + 2 * slot_b) + local % 2, owner % 2


def kernel(
    fwd_idx, bwd_idx, rhs_hbm, inv_hbm, low_hbm, out_ref,
    rhs, inv, low, low_hi, low_lo, fwd, own_part, gath_0, gath_1, gath_2, part, col_in, rest,
    sol, terms_0, terms_1, terms_2, others_0, others_1, others_2, own, up_a, dn_a, row_x, in_x, mid_l, mid_r, fin_l, fin_r, col_z, in_z,
    load_sem, send_sem, inv_sem, ag_sem, rs_sem, col_sem,
):
    gath, terms = (gath_0, gath_1, gath_2), (terms_0, terms_1, terms_2)
    others = (others_0, others_1, others_2)
    row, c = lax.axis_index("row"), lax.axis_index("col")
    z, x, core = row // (2 * NX), row // 2 % NX, row % 2

    def at_row(zz, xx, cc):
        return ((zz * NX + xx) * 2 + cc, c)

    z_dev = [None] + [at_row((z + a) % NZ, x, core) for a in range(1, NZ)]
    x_rt, x_lf = at_row(z, (x + 1) % NX, core), at_row(z, (x + NX - 1) % NX, core)
    x_far = at_row(z, (x + 2) % NX, core)
    x_dev = [None, x_rt, x_far, x_lf]
    sib = at_row(z, x, 1 - core)
    col_dev = [None] + [(row, (c + t) % 4) for t in (1, 2, 3)]

    loads = [
        pltpu.make_async_copy(inv_hbm, inv.at[:, :, c], load_sem.at[0]),
        pltpu.make_async_copy(rhs_hbm.at[0], rhs.at[0], load_sem.at[1]),
        pltpu.make_async_copy(rhs_hbm.at[pl.ds(1, 3)], rhs.at[pl.ds(1, 3)], load_sem.at[2]),
        pltpu.make_async_copy(low_hbm, low, load_sem.at[3]),
    ]
    for load in loads:
        load.start()

    barrier = pltpu.get_barrier_semaphore()
    partners = [z_dev[a] for a in (1, 2, 3, 5, 6, 7)] + x_dev[1:] + [sib] + col_dev[1:]
    for partner in partners:
        pl.semaphore_signal(barrier, inc=1, device_id=partner, device_id_type=MESH)

    for level in range(3):
        terms[level][64] = jnp.zeros((32, 128), jnp.float32)
        others[level][64] = jnp.zeros((32, 128), jnp.float32)
    loads[0].wait()
    loads[1].wait()
    for j in range(4):
        fwd[0, j] = exact_dot(inv[0, j, c], rhs[0, j])
    pl.semaphore_wait(barrier, len(partners))

    def put(src, dst, sem, device, out_sem):
        pltpu.make_async_remote_copy(
            src_ref=src, dst_ref=dst, send_sem=out_sem, recv_sem=sem, device_id=device, device_id_type=MESH
        ).start()

    def take(dst, sem, device=None):
        pltpu.make_async_remote_copy(
            src_ref=dst, dst_ref=dst, send_sem=send_sem.at[0], recv_sem=sem, device_id=sib, device_id_type=MESH
        ).wait_recv()

    def sent(count, out_sem):
        ref = gath[0].at[pl.ds(0, count)]
        pltpu.make_async_remote_copy(
            src_ref=ref, dst_ref=ref, send_sem=out_sem, recv_sem=out_sem, device_id=sib, device_id_type=MESH
        ).wait_send()

    def gather_row(level, ready, between):
        g_sem = send_sem.at[0]
        sib_sem = ag_sem.at[level, 95]
        issued = set()

        def ref(half, slot, count, plane=0):
            return gath[level].at[pl.ds(128 * plane + 64 * half + 2 * slot, 2 * count)]

        def share(half, slot, count):
            put(ref(half, slot, count), ref(half, slot, count, 1), sib_sem, sib, g_sem)

        def issue(arrived, halves):
            for number, (half, dz, dx, src, dst, count, needs) in enumerate(ROUTES):
                if number in issued or half not in halves or any(need >= arrived for need in needs):
                    continue
                issued.add(number)
                device = z_dev[dz % NZ] if dz else x_dev[dx % NX]
                put(ref(half, src, count), ref(half, dst, count), ag_sem.at[level, number], device, g_sem)

        for half in (0, 1):
            ready(level, half)
            gath[level][pl.ds(64 * half, 2)] = fwd[level, pl.ds(2 * half, 2)]
            issue(0, range(half + 1))
            share(half, 0, 1)
        between()
        for number, (half, dz, dx, src, dst, count, needs) in enumerate(ROUTES):
            take(ref(half, dst, count), ag_sem.at[level, number])
            issue(number + 1, (0, 1))
            share(half, dst, count)
        take(gath[level].at[pl.ds(128, 128)], sib_sem)
        sent(2 * sum(route[5] for route in ROUTES) + 128, g_sem)

    def reduce_row(low_level, build):
        r_sem = send_sem.at[0]
        ids = {}

        def sem(key):
            return rs_sem.at[low_level, ids.setdefault(key, len(ids))]

        def own_a(a, p):
            return own.at[low_level, pl.ds(2 * (a * NX + p), 2)]

        def own_b(pos, zpos, count):
            return own.at[low_level, pl.ds(64 + 2 * (pos * NZ + zpos), 2 * count)]

        def ref_az(hops, p, direction):
            return (up_a if direction == 1 else dn_a).at[low_level, hops, p]

        def send_az(src, hops, p, direction, step=1):
            slot = hops - step if step == 1 else 3
            put(src, ref_az(slot, p, direction), sem(("az", slot, p, direction)), z_dev[direction * step % NZ], r_sem)

        def pass_az(hops, p, direction):
            ref = ref_az(hops, p, direction)
            take(ref, sem(("az", hops, p, direction)))
            if hops == 2 and (p < 2) == (direction == 1):
                far = ref_az(3, p, direction)
                take(far, sem(("az", 3, p, direction)))
                ref[...] += own_a(direction * hops % NZ, p)[...] + far[...]
                send_az(ref, hops, p, direction)
            elif hops:
                ref[...] += own_a(direction * hops % NZ, p)[...]
                send_az(ref, hops, p, direction)

        zs = [(7, 1), (3, 4), (0, 3)]

        def mid(buffer, part_no):
            zpos, count = zs[part_no]
            return buffer.at[low_level, pl.ds(2 * zpos, 2 * count)]

        build(112, 16)
        put(own_b(3, 7, 1), mid(mid_l, 0), sem(("m", 0)), x_rt, r_sem)
        put(own_b(3, 3, 4), mid(mid_r, 1), sem(("m", 1)), x_lf, r_sem)
        put(own_b(3, 0, 3), mid(mid_l, 2), sem(("m", 2)), x_rt, r_sem)
        build(24, 24)
        for p in (3, 1, 2, 0):
            send_az(own_a(4, p), 4, p, 1 if p < 2 else -1, 2)
            send_az(own_a(3, p), 3, p, 1)
            send_az(own_a(5, p), 3, p, -1)
        build(80, 32)
        put(own_b(2, 7, 1), mid(fin_r, 0), sem(("fr", 0)), x_lf, r_sem)
        put(own_b(1, 3, 4), mid(fin_l, 1), sem(("fl", 1)), x_rt, r_sem)
        put(own_b(2, 0, 3), mid(fin_r, 2), sem(("fr", 2)), x_lf, r_sem)
        build(0, 24)
        build(48, 32)

        take(mid(mid_l, 0), sem(("m", 0)))
        mid(mid_l, 0)[...] += own_b(1, 7, 1)[...]
        put(mid(mid_l, 0), mid(fin_l, 0), sem(("fl", 0)), x_rt, r_sem)
        take(mid(mid_r, 1), sem(("m", 1)))
        mid(mid_r, 1)[...] += own_b(2, 3, 4)[...]
        put(mid(mid_r, 1), mid(fin_r, 1), sem(("fr", 1)), x_lf, r_sem)
        for p in (3, 1):
            pass_az(2, p, 1)
            pass_az(2, p, -1)
        take(mid(mid_l, 2), sem(("m", 2)))
        mid(mid_l, 2)[...] += own_b(1, 0, 3)[...]
        put(mid(mid_l, 2), mid(fin_l, 2), sem(("fl", 2)), x_rt, r_sem)
        for p in (2, 0):
            pass_az(2, p, 1)
            pass_az(2, p, -1)

        def finish_x(part_no):
            zpos, count = zs[part_no]
            take(mid(fin_l, part_no), sem(("fl", part_no)))
            take(mid(fin_r, part_no), sem(("fr", part_no)))
            col_z[low_level, pl.ds(2 * zpos, 2 * count)] = (
                own_b(0, zpos, count)[...] + mid(fin_l, part_no)[...] + mid(fin_r, part_no)[...]
            )

        def z_part(a):
            return col_z.at[low_level, pl.ds(2 * Z_POS[a], 2)]

        def send_bz(src, key, hops):
            put(src, in_z.at[low_level, key], sem(("bz", key)), z_dev[hops % NZ], r_sem)

        def got_bz(key):
            take(in_z.at[low_level, key], sem(("bz", key)))
            return in_z[low_level, key]

        finish_x(0)
        send_bz(z_part(4), 0, 2)
        for p in (3, 1):
            pass_az(1, p, 1)
            pass_az(1, p, -1)
        finish_x(1)
        send_bz(z_part(3), 1, 1)
        send_bz(z_part(5), 2, -1)
        finish_x(2)
        send_bz(z_part(1), 5, 1)
        send_bz(z_part(7), 6, -1)
        for p in (2, 0):
            pass_az(1, p, 1)
            pass_az(1, p, -1)
        z_part(2)[...] += got_bz(0) + got_bz(1)
        send_bz(z_part(2), 3, 2)
        z_part(6)[...] += got_bz(2)
        send_bz(z_part(6), 4, -2)
        for p in (3, 1, 2, 0):
            pass_az(0, p, 1)
            pass_az(0, p, -1)
            row_x[low_level, p] = own_a(0, p)[...] + up_a[low_level, 0, p] + dn_a[low_level, 0, p]
            if p:
                device = (None, x_rt, x_lf, x_far)[p]
                put(row_x.at[low_level, p], in_x.at[low_level, p - 1], sem(("x", p)), device, r_sem)
        half_b = col_z[low_level, pl.ds(0, 2)]
        for key in (5, 6, 3, 4):
            half_b = half_b + got_bz(key)
        start_solve(low_level, 1, fwd[low_level, pl.ds(2, 2)] - half_b)
        for p in (1, 3, 2):
            take(in_x.at[low_level, p - 1], sem(("x", p)))
        half_a = (
            row_x[low_level, 0] + in_x[low_level, 0] + in_x[low_level, 1] + in_x[low_level, 2]
        )
        start_solve(low_level, 0, fwd[low_level, pl.ds(0, 2)] - half_a)
        sent(188, r_sem)

    for level in (1, 2, 3, 0):
        for t in (1, 2, 3):
            ref = inv.at[level, :, c]
            put(ref, ref, inv_sem.at[level, t - 1], col_dev[t], send_sem.at[1])

    def whole_inv(level):
        for t in (1, 2, 3):
            take(inv.at[level, :, 0], inv_sem.at[level, t - 1])

    def forward_level(low_level):
        level = low_level + 1

        def between():
            if low_level == 0:
                loads[2].wait()
                loads[3].wait()

            for j in range(4):
                own_part[j] = exact_dot(inv[level, j, c], rhs[level, j])
            for j in range(4):
                low_hi[j], low_lo[j] = split(low[low_level, j].T)

        gather_row(low_level, finish_forward, between)
        whole_inv(level)
        for half in (0, 1):
            for j in (2 * half, 2 * half + 1):
                picked = jnp.concatenate(
                    [gath[low_level][fwd_idx[low_level, 4 * core + j, d]] for d in range(16)], axis=0
                )
                update = split_dot((low_hi[j], low_lo[j]), split(picked))
                done = exact_dot(inv[level, j].reshape(128, 128), update)
                for piece in range(4):
                    part[low_level, piece, j] = done[32 * piece : 32 * piece + 32]
            for t in (2, 1, 3):
                put(
                    part.at[low_level, (c + t) % 4, pl.ds(2 * half, 2)],
                    col_in.at[low_level, t - 1, pl.ds(2 * half, 2)],
                    col_sem.at[low_level, half, t - 1], col_dev[t], send_sem.at[2],
                )

    def finish_forward(level, half):
        if level == 0:
            return
        blocks = pl.ds(2 * half, 2)
        total = own_part[blocks] - part[level - 1, c, blocks]
        for t in (1, 3, 2):
            take(col_in.at[level - 1, t - 1, blocks], col_sem.at[level - 1, half, t - 1])
            total = total - col_in[level - 1, t - 1, blocks]
        fwd[level, blocks] = total

    for low_level in range(3):
        forward_level(low_level)
    whole_inv(0)

    def start_solve(level, half, value):
        blocks = pl.ds(2 * half, 2)
        rest[level, c, blocks] = value
        ref = rest.at[level, c, blocks]
        for t in (2, 1, 3):
            put(ref, ref, col_sem.at[3 + level, half, t - 1], col_dev[t], send_sem.at[2])

    def finish_solve(level, half, product):
        blocks = pl.ds(2 * half, 2)
        for t in (1, 3, 2):
            take(rest.at[level, c, blocks], col_sem.at[3 + level, half, t - 1])
        for j in (2 * half, 2 * half + 1):
            whole = inv[level, j].reshape(128, 128)
            sol[j] = exact_dot(whole.T, rest[level, :, j].reshape(128, 128))
            product(j)
            out_ref[level, j] = sol[j, pl.ds(pl.multiple_of(32 * c, 32), 32), :]

    for half in (1, 0):
        finish_forward(3, half)
        start_solve(3, half, fwd[3, pl.ds(2 * half, 2)])

    def backward_level(low_level):
        t_sem = rs_sem.at[low_level, 95]

        def product(j):
            value = exact_dot(low[low_level, j], sol[j])
            terms[low_level][pl.ds(16 * j, 16)] = value.reshape(16, 32, 128)
            put(
                terms[low_level].at[pl.ds(16 * j, 16)], others[low_level].at[pl.ds(16 * j, 16)],
                t_sem, sib, send_sem.at[0],
            )

        finish_solve(low_level + 1, 1, product)
        finish_solve(low_level + 1, 0, product)

        def build_mine(place, inner):
            own[low_level, place] = (
                terms[low_level][bwd_idx[low_level, place]]
                + terms[low_level][bwd_idx[low_level, 128 + place]]
            )
            return inner

        def build_other(place, inner):
            own[low_level, place] += (
                others[low_level][bwd_idx[low_level, 256 + place]]
                + others[low_level][bwd_idx[low_level, 384 + place]]
            )
            return inner

        lax.fori_loop(0, 128, build_mine, 0, unroll=8)
        take(others[low_level].at[pl.ds(0, 64)], t_sem)

        def build(first, count):
            lax.fori_loop(first, first + count, build_other, 0, unroll=8)

        reduce_row(low_level, build)

    for low_level in (2, 1, 0):
        backward_level(low_level)
    for half in (1, 0):
        finish_solve(0, half, lambda j: None)
    sent(48, send_sem.at[1])
    sent(84, send_sem.at[2])


def on_device(right_sides, inverse_diag, lower_blocks, depends_on):
    row = lax.axis_index("row")
    z, x, core = row // (2 * NX), row // 2 % NX, row % 2
    wanted = lax.dynamic_slice(depends_on, (0, 4 * (row - core), 0), (3, 8, 16))
    place, owner_core = block_place(wanted, lambda zz: z - zz, lambda xx: x - xx)
    fwd_idx = place + jnp.where(owner_core == core, 0, 128)
    place, owner_core = block_place(wanted, lambda zz: zz - z, lambda xx: xx - x)
    place = jnp.where(owner_core == core, place, -1)
    match = place[:, :, :, None] == jnp.arange(128, dtype=jnp.int32)
    entry = 16 * (jnp.arange(8, dtype=jnp.int32) % 4)[:, None] + jnp.arange(16, dtype=jnp.int32)
    owner = (jnp.arange(8, dtype=jnp.int32) // 4)[:, None]
    lists = []
    for source in (core, 1 - core):
        found = match & (owner == source)[:, :, None]
        first = jnp.min(jnp.where(found, entry[:, :, None], 64), axis=(1, 2))
        last = jnp.max(jnp.where(found, entry[:, :, None], -1), axis=(1, 2))
        lists.append(first)
        lists.append(jnp.where(last > first, last, 64))
    bwd_idx = jnp.concatenate(lists, axis=1)

    f32 = jnp.float32

    def vmem(*shape):
        return pltpu.VMEM(shape, f32)

    any_spec = pl.BlockSpec(memory_space=pl.ANY)
    smem_spec = pl.BlockSpec(memory_space=pltpu.SMEM)
    block = (32, 128)
    return pl.pallas_call(
        kernel,
        out_shape=jax.ShapeDtypeStruct((4, 4, 32, 128), f32),
        in_specs=[smem_spec, smem_spec, any_spec, any_spec, any_spec],
        out_specs=pl.BlockSpec(memory_space=pltpu.VMEM),
        scratch_shapes=[
            vmem(4, 4, 128, 128),
            vmem(4, 4, 4, *block),
            vmem(3, 4, 512, 128),
            pltpu.VMEM((4, 128, 512), jnp.bfloat16),
            pltpu.VMEM((4, 128, 512), jnp.bfloat16),
            vmem(4, 4, *block),
            vmem(4, *block),
            vmem(256, *block),
            vmem(256, *block),
            vmem(256, *block),
            vmem(3, 4, 4, *block),
            vmem(3, 3, 4, *block),
            vmem(4, 4, 4, *block),
            vmem(4, 128, 128),
            vmem(65, *block),
            vmem(65, *block),
            vmem(65, *block),
            vmem(65, *block),
            vmem(65, *block),
            vmem(65, *block),
            vmem(3, 128, *block),
            vmem(3, 4, 4, 2, *block),
            vmem(3, 4, 4, 2, *block),
            vmem(3, 4, 2, *block),
            vmem(3, 3, 2, *block),
            vmem(3, 16, *block),
            vmem(3, 16, *block),
            vmem(3, 16, *block),
            vmem(3, 16, *block),
            vmem(3, 16, *block),
            vmem(3, 7, 2, *block),
            pltpu.SemaphoreType.DMA((4,)),
            pltpu.SemaphoreType.DMA((3,)),
            pltpu.SemaphoreType.DMA((4, 3)),
            pltpu.SemaphoreType.DMA((3, 96)),
            pltpu.SemaphoreType.DMA((3, 96)),
            pltpu.SemaphoreType.DMA((7, 2, 3)),
        ],
        compiler_params=pltpu.CompilerParams(
            collective_id=0, has_side_effects=True, vmem_limit_bytes=60 * 1024 * 1024
        ),
    )(fwd_idx, bwd_idx, right_sides, inverse_diag, lower_blocks.reshape(3, 4, 512, 128))


def solution(mesh):
    return jax.shard_map(
        on_device,
        mesh=mesh,
        in_specs=(
            P(None, "row", None, None),
            P(None, "row", "col", None),
            P(None, "row", None, "col", None),
            P(),
        ),
        out_specs=P(None, "row", "col", None),
        check_vma=False,
    )
```

```python
import jax
import jax.numpy as jnp
from jax import lax
from jax.experimental import pallas as pl
from jax.experimental.pallas import tpu as pltpu
from jax.sharding import PartitionSpec as P

MESH = pl.DeviceIdType.MESH
NZ, NX = 8, 4
Z_POS = {0: 0, 1: 1, 7: 2, 2: 3, 6: 4, 3: 5, 5: 6, 4: 7}
ROUTES = (
    (0, 0, 1, 0, 1, 1, ()),
    (0, 0, -1, 0, 2, 1, ()),
    (0, 1, 0, 0, 4, 1, ()),
    (0, -1, 0, 0, 28, 1, ()),
    (0, 0, 2, 0, 3, 1, ()),
    (1, 1, 0, 0, 1, 1, ()),
    (1, -1, 0, 0, 2, 1, ()),
    (1, 0, -1, 0, 16, 1, ()),
    (1, 0, 1, 0, 8, 1, ()),
    (1, 3, 0, 0, 5, 1, ()),
    (1, -3, 0, 0, 6, 1, ()),
    (0, 1, 0, 1, 5, 1, (0,)),
    (0, -1, 0, 1, 29, 1, (0,)),
    (0, 1, 0, 2, 6, 1, (1,)),
    (0, -1, 0, 2, 30, 1, (1,)),
    (0, 1, 0, 4, 8, 1, (2,)),
    (0, -1, 0, 28, 24, 1, (3,)),
    (1, 0, 1, 1, 9, 2, (5, 6)),
    (1, 0, -1, 1, 17, 2, (5, 6)),
    (0, 1, 0, 3, 7, 1, (4,)),
    (0, -1, 0, 3, 31, 1, (4,)),
    (1, 0, 1, 8, 24, 1, (8,)),
    (1, 1, 0, 1, 3, 1, (5,)),
    (1, -1, 0, 2, 4, 1, (6,)),
    (1, 1, 0, 5, 7, 1, (9,)),
    (0, -1, 0, 29, 25, 1, (12,)),
    (1, 0, 1, 5, 13, 2, (9, 10)),
    (1, 0, -1, 5, 21, 2, (9, 10)),
    (0, 1, 0, 5, 9, 1, (11,)),
    (0, -1, 0, 30, 26, 1, (14,)),
    (0, 1, 0, 6, 10, 1, (13,)),
    (0, -1, 0, 24, 20, 1, (16,)),
    (0, 1, 0, 8, 12, 1, (15,)),
    (0, -1, 0, 31, 27, 1, (20,)),
    (1, 0, -1, 17, 25, 2, (18,)),
    (0, 2, 0, 8, 16, 1, (15,)),
    (1, 0, 1, 3, 11, 2, (22, 23)),
    (1, 0, -1, 3, 19, 2, (22, 23)),
    (0, -1, 0, 25, 21, 1, (25,)),
    (0, 1, 0, 7, 11, 1, (19,)),
    (1, 0, 1, 7, 15, 1, (24,)),
    (1, 0, -1, 7, 23, 1, (24,)),
    (0, -1, 0, 26, 22, 1, (29,)),
    (0, 1, 0, 9, 13, 1, (28,)),
    (1, 0, -1, 21, 29, 2, (27,)),
    (0, -2, 0, 26, 18, 1, (29,)),
    (0, 2, 0, 9, 17, 1, (28,)),
    (0, -1, 0, 27, 23, 1, (33,)),
    (0, 1, 0, 10, 14, 1, (30,)),
    (0, 1, 0, 11, 15, 1, (39,)),
    (1, 0, 1, 11, 27, 2, (36,)),
    (0, -2, 0, 27, 19, 1, (33,)),
    (1, 0, 1, 15, 31, 1, (40,)),
)


def split(v):
    high = v.astype(jnp.bfloat16)
    return high, (v - high.astype(jnp.float32)).astype(jnp.bfloat16)


def split_dot(a, b):
    def dot(u, v):
        return jnp.dot(u, v, preferred_element_type=jnp.float32)

    return dot(a[0], b[0]) + (dot(a[0], b[1]) + dot(a[1], b[0]))


def exact_dot(a, b):
    return split_dot(split(a), split(b))


def ring_pos(distance, size):
    return jnp.where(
        distance == 0,
        0,
        jnp.where(distance <= size // 2, 2 * distance - 1, 2 * (size - distance)),
    )


def block_place(block, z_of, x_of):
    owner, local = block // 4, block % 4
    a = z_of(owner // (2 * NX)) % NZ
    b = x_of(owner // 2 % NX) % NX
    slot_a = a * NX + ring_pos(b, NX)
    slot_b = ring_pos(b, NX) * NZ + ring_pos(a, NZ)
    return jnp.where(local < 2, 2 * slot_a, 64 + 2 * slot_b) + local % 2, owner % 2


def kernel(
    fwd_idx, bwd_idx, rhs_hbm, inv_hbm, low_hbm, out_ref,
    rhs, inv, low, low_hi, low_lo, fwd, own_part, gath_0, gath_1, gath_2, part, col_in, rest,
    sol, terms_0, terms_1, terms_2, others_0, others_1, others_2, own, up_a, dn_a, row_x, in_x, mid_l, mid_r, fin_l, fin_r, col_z, in_z,
    load_sem, send_sem, inv_sem, ag_sem, rs_sem, col_sem,
):
    gath, terms = (gath_0, gath_1, gath_2), (terms_0, terms_1, terms_2)
    others = (others_0, others_1, others_2)
    row, c = lax.axis_index("row"), lax.axis_index("col")
    z, x, core = row // (2 * NX), row // 2 % NX, row % 2

    def at_row(zz, xx, cc):
        return ((zz * NX + xx) * 2 + cc, c)

    z_dev = [None] + [at_row((z + a) % NZ, x, core) for a in range(1, NZ)]
    x_rt, x_lf = at_row(z, (x + 1) % NX, core), at_row(z, (x + NX - 1) % NX, core)
    x_far = at_row(z, (x + 2) % NX, core)
    x_dev = [None, x_rt, x_far, x_lf]
    sib = at_row(z, x, 1 - core)
    col_dev = [None] + [(row, (c + t) % 4) for t in (1, 2, 3)]

    loads = [
        pltpu.make_async_copy(inv_hbm, inv.at[:, :, c], load_sem.at[0]),
        pltpu.make_async_copy(rhs_hbm.at[0], rhs.at[0], load_sem.at[1]),
        pltpu.make_async_copy(rhs_hbm.at[pl.ds(1, 3)], rhs.at[pl.ds(1, 3)], load_sem.at[2]),
        pltpu.make_async_copy(low_hbm, low, load_sem.at[3]),
    ]
    for load in loads:
        load.start()

    barrier = pltpu.get_barrier_semaphore()
    partners = [z_dev[a] for a in (1, 2, 3, 5, 6, 7)] + x_dev[1:] + [sib] + col_dev[1:]
    for partner in partners:
        pl.semaphore_signal(barrier, inc=1, device_id=partner, device_id_type=MESH)

    for level in range(3):
        terms[level][64] = jnp.zeros((32, 128), jnp.float32)
        others[level][64] = jnp.zeros((32, 128), jnp.float32)
    loads[0].wait()
    loads[1].wait()
    for j in range(4):
        fwd[0, j] = exact_dot(inv[0, j, c], rhs[0, j])
    pl.semaphore_wait(barrier, len(partners))

    def put(src, dst, sem, device, out_sem):
        pltpu.make_async_remote_copy(
            src_ref=src, dst_ref=dst, send_sem=out_sem, recv_sem=sem, device_id=device, device_id_type=MESH
        ).start()

    def take(dst, sem, device=None):
        pltpu.make_async_remote_copy(
            src_ref=dst, dst_ref=dst, send_sem=send_sem.at[0], recv_sem=sem, device_id=sib, device_id_type=MESH
        ).wait_recv()

    def sent(count, out_sem):
        ref = gath[0].at[pl.ds(0, count)]
        pltpu.make_async_remote_copy(
            src_ref=ref, dst_ref=ref, send_sem=out_sem, recv_sem=out_sem, device_id=sib, device_id_type=MESH
        ).wait_send()

    def gather_row(level, ready, between):
        g_sem = send_sem.at[level]
        sib_sem = ag_sem.at[level, 95]
        issued = set()

        def ref(half, slot, count, plane=0):
            return gath[level].at[pl.ds(128 * plane + 64 * half + 2 * slot, 2 * count)]

        def share(half, slot, count):
            put(ref(half, slot, count), ref(half, slot, count, 1), sib_sem, sib, g_sem)

        def issue(arrived, halves):
            for number, (half, dz, dx, src, dst, count, needs) in enumerate(ROUTES):
                if number in issued or half not in halves or any(need >= arrived for need in needs):
                    continue
                issued.add(number)
                device = z_dev[dz % NZ] if dz else x_dev[dx % NX]
                put(ref(half, src, count), ref(half, dst, count), ag_sem.at[level, number], device, g_sem)

        for half in (0, 1):
            ready(level, half)
            gath[level][pl.ds(64 * half, 2)] = fwd[level, pl.ds(2 * half, 2)]
            issue(0, range(half + 1))
            share(half, 0, 1)
        between()
        for number, (half, dz, dx, src, dst, count, needs) in enumerate(ROUTES):
            take(ref(half, dst, count), ag_sem.at[level, number])
            issue(number + 1, (0, 1))
            share(half, dst, count)
        take(gath[level].at[pl.ds(128, 128)], sib_sem)

    def reduce_row(low_level, build):
        r_sem = send_sem.at[3 + low_level]
        ids = {}

        def sem(key):
            return rs_sem.at[low_level, ids.setdefault(key, len(ids))]

        def own_a(a, p):
            return own.at[low_level, pl.ds(2 * (a * NX + p), 2)]

        def own_b(pos, zpos, count):
            return own.at[low_level, pl.ds(64 + 2 * (pos * NZ + zpos), 2 * count)]

        def ref_az(hops, p, direction):
            return (up_a if direction == 1 else dn_a).at[low_level, hops, p]

        def send_az(src, hops, p, direction, step=1):
            slot = hops - step if step == 1 else 3
            put(src, ref_az(slot, p, direction), sem(("az", slot, p, direction)), z_dev[direction * step % NZ], r_sem)

        def pass_az(hops, p, direction):
            ref = ref_az(hops, p, direction)
            take(ref, sem(("az", hops, p, direction)))
            if hops == 2 and (p < 2) == (direction == 1):
                far = ref_az(3, p, direction)
                take(far, sem(("az", 3, p, direction)))
                ref[...] += own_a(direction * hops % NZ, p)[...] + far[...]
                send_az(ref, hops, p, direction)
            elif hops:
                ref[...] += own_a(direction * hops % NZ, p)[...]
                send_az(ref, hops, p, direction)

        zs = [(7, 1), (3, 4), (0, 3)]

        def mid(buffer, part_no):
            zpos, count = zs[part_no]
            return buffer.at[low_level, pl.ds(2 * zpos, 2 * count)]

        build(112, 16)
        put(own_b(3, 7, 1), mid(mid_l, 0), sem(("m", 0)), x_rt, r_sem)
        put(own_b(3, 3, 4), mid(mid_r, 1), sem(("m", 1)), x_lf, r_sem)
        put(own_b(3, 0, 3), mid(mid_l, 2), sem(("m", 2)), x_rt, r_sem)
        build(24, 24)
        for p in (3, 1, 2, 0):
            send_az(own_a(4, p), 4, p, 1 if p < 2 else -1, 2)
            send_az(own_a(3, p), 3, p, 1)
            send_az(own_a(5, p), 3, p, -1)
        build(80, 32)
        put(own_b(2, 7, 1), mid(fin_r, 0), sem(("fr", 0)), x_lf, r_sem)
        put(own_b(1, 3, 4), mid(fin_l, 1), sem(("fl", 1)), x_rt, r_sem)
        put(own_b(2, 0, 3), mid(fin_r, 2), sem(("fr", 2)), x_lf, r_sem)
        build(0, 24)
        build(48, 32)

        take(mid(mid_l, 0), sem(("m", 0)))
        mid(mid_l, 0)[...] += own_b(1, 7, 1)[...]
        put(mid(mid_l, 0), mid(fin_l, 0), sem(("fl", 0)), x_rt, r_sem)
        take(mid(mid_r, 1), sem(("m", 1)))
        mid(mid_r, 1)[...] += own_b(2, 3, 4)[...]
        put(mid(mid_r, 1), mid(fin_r, 1), sem(("fr", 1)), x_lf, r_sem)
        for p in (3, 1):
            pass_az(2, p, 1)
            pass_az(2, p, -1)
        take(mid(mid_l, 2), sem(("m", 2)))
        mid(mid_l, 2)[...] += own_b(1, 0, 3)[...]
        put(mid(mid_l, 2), mid(fin_l, 2), sem(("fl", 2)), x_rt, r_sem)
        for p in (2, 0):
            pass_az(2, p, 1)
            pass_az(2, p, -1)

        def finish_x(part_no):
            zpos, count = zs[part_no]
            take(mid(fin_l, part_no), sem(("fl", part_no)))
            take(mid(fin_r, part_no), sem(("fr", part_no)))
            col_z[low_level, pl.ds(2 * zpos, 2 * count)] = (
                own_b(0, zpos, count)[...] + mid(fin_l, part_no)[...] + mid(fin_r, part_no)[...]
            )

        def z_part(a):
            return col_z.at[low_level, pl.ds(2 * Z_POS[a], 2)]

        def send_bz(src, key, hops):
            put(src, in_z.at[low_level, key], sem(("bz", key)), z_dev[hops % NZ], r_sem)

        def got_bz(key):
            take(in_z.at[low_level, key], sem(("bz", key)))
            return in_z[low_level, key]

        finish_x(0)
        send_bz(z_part(4), 0, 2)
        for p in (3, 1):
            pass_az(1, p, 1)
            pass_az(1, p, -1)
        finish_x(1)
        send_bz(z_part(3), 1, 1)
        send_bz(z_part(5), 2, -1)
        finish_x(2)
        send_bz(z_part(1), 5, 1)
        send_bz(z_part(7), 6, -1)
        for p in (2, 0):
            pass_az(1, p, 1)
            pass_az(1, p, -1)
        z_part(2)[...] += got_bz(0) + got_bz(1)
        send_bz(z_part(2), 3, 2)
        z_part(6)[...] += got_bz(2)
        send_bz(z_part(6), 4, -2)
        for p in (3, 1, 2, 0):
            pass_az(0, p, 1)
            pass_az(0, p, -1)
            row_x[low_level, p] = own_a(0, p)[...] + up_a[low_level, 0, p] + dn_a[low_level, 0, p]
            if p:
                device = (None, x_rt, x_lf, x_far)[p]
                put(row_x.at[low_level, p], in_x.at[low_level, p - 1], sem(("x", p)), device, r_sem)
        half_b = col_z[low_level, pl.ds(0, 2)]
        for key in (5, 6, 3, 4):
            half_b = half_b + got_bz(key)
        start_solve(low_level, 1, fwd[low_level, pl.ds(2, 2)] - half_b)
        for p in (1, 3, 2):
            take(in_x.at[low_level, p - 1], sem(("x", p)))
        half_a = (
            row_x[low_level, 0] + in_x[low_level, 0] + in_x[low_level, 1] + in_x[low_level, 2]
        )
        start_solve(low_level, 0, fwd[low_level, pl.ds(0, 2)] - half_a)

    for level in (1, 2, 3, 0):
        for t in (1, 2, 3):
            ref = inv.at[level, :, c]
            put(ref, ref, inv_sem.at[level, t - 1], col_dev[t], send_sem.at[6])

    def whole_inv(level):
        for t in (1, 2, 3):
            take(inv.at[level, :, 0], inv_sem.at[level, t - 1])

    def forward_level(low_level):
        level = low_level + 1

        def between():
            if low_level == 0:
                loads[2].wait()
                loads[3].wait()

            for j in range(4):
                own_part[j] = exact_dot(inv[level, j, c], rhs[level, j])
            for j in range(4):
                low_hi[j], low_lo[j] = split(low[low_level, j].T)

        gather_row(low_level, finish_forward, between)
        whole_inv(level)
        for half in (0, 1):
            for j in (2 * half, 2 * half + 1):
                picked = jnp.concatenate(
                    [gath[low_level][fwd_idx[low_level, 4 * core + j, d]] for d in range(16)], axis=0
                )
                update = split_dot((low_hi[j], low_lo[j]), split(picked))
                done = exact_dot(inv[level, j].reshape(128, 128), update)
                for piece in range(4):
                    part[low_level, piece, j] = done[32 * piece : 32 * piece + 32]
            for t in (2, 1, 3):
                put(
                    part.at[low_level, (c + t) % 4, pl.ds(2 * half, 2)],
                    col_in.at[low_level, t - 1, pl.ds(2 * half, 2)],
                    col_sem.at[low_level, half, t - 1], col_dev[t], send_sem.at[7],
                )

    def finish_forward(level, half):
        if level == 0:
            return
        blocks = pl.ds(2 * half, 2)
        total = own_part[blocks] - part[level - 1, c, blocks]
        for t in (1, 3, 2):
            take(col_in.at[level - 1, t - 1, blocks], col_sem.at[level - 1, half, t - 1])
            total = total - col_in[level - 1, t - 1, blocks]
        fwd[level, blocks] = total

    for low_level in range(3):
        forward_level(low_level)
    whole_inv(0)

    def start_solve(level, half, value):
        blocks = pl.ds(2 * half, 2)
        rest[level, c, blocks] = value
        ref = rest.at[level, c, blocks]
        for t in (2, 1, 3):
            put(ref, ref, col_sem.at[3 + level, half, t - 1], col_dev[t], send_sem.at[7])

    def finish_solve(level, half, product):
        blocks = pl.ds(2 * half, 2)
        for t in (1, 3, 2):
            take(rest.at[level, c, blocks], col_sem.at[3 + level, half, t - 1])
        for j in (2 * half, 2 * half + 1):
            whole = inv[level, j].reshape(128, 128)
            sol[j] = exact_dot(whole.T, rest[level, :, j].reshape(128, 128))
            product(j)
            out_ref[level, j] = sol[j, pl.ds(pl.multiple_of(32 * c, 32), 32), :]

    for half in (1, 0):
        finish_forward(3, half)
        start_solve(3, half, fwd[3, pl.ds(2 * half, 2)])

    def backward_level(low_level):
        t_sem = rs_sem.at[low_level, 95]

        def product(j):
            value = exact_dot(low[low_level, j], sol[j])
            terms[low_level][pl.ds(16 * j, 16)] = value.reshape(16, 32, 128)
            put(
                terms[low_level].at[pl.ds(16 * j, 16)], others[low_level].at[pl.ds(16 * j, 16)],
                t_sem, sib, send_sem.at[3 + low_level],
            )

        finish_solve(low_level + 1, 1, product)
        finish_solve(low_level + 1, 0, product)

        def build_mine(place, inner):
            own[low_level, place] = (
                terms[low_level][bwd_idx[low_level, place]]
                + terms[low_level][bwd_idx[low_level, 128 + place]]
            )
            return inner

        def build_other(place, inner):
            own[low_level, place] += (
                others[low_level][bwd_idx[low_level, 256 + place]]
                + others[low_level][bwd_idx[low_level, 384 + place]]
            )
            return inner

        lax.fori_loop(0, 128, build_mine, 0, unroll=8)
        take(others[low_level].at[pl.ds(0, 64)], t_sem)

        def build(first, count):
            lax.fori_loop(first, first + count, build_other, 0, unroll=8)

        reduce_row(low_level, build)

    for low_level in (2, 1, 0):
        backward_level(low_level)
    for half in (1, 0):
        finish_solve(0, half, lambda j: None)
    sent(48, send_sem.at[6])
    sent(84, send_sem.at[7])
    for level in range(3):
        sent(2 * sum(route[5] for route in ROUTES) + 128, send_sem.at[level])
        sent(188, send_sem.at[3 + level])


def on_device(right_sides, inverse_diag, lower_blocks, depends_on):
    row = lax.axis_index("row")
    z, x, core = row // (2 * NX), row // 2 % NX, row % 2
    wanted = lax.dynamic_slice(depends_on, (0, 4 * (row - core), 0), (3, 8, 16))
    place, owner_core = block_place(wanted, lambda zz: z - zz, lambda xx: x - xx)
    fwd_idx = place + jnp.where(owner_core == core, 0, 128)
    place, owner_core = block_place(wanted, lambda zz: zz - z, lambda xx: xx - x)
    place = jnp.where(owner_core == core, place, -1)
    match = place[:, :, :, None] == jnp.arange(128, dtype=jnp.int32)
    entry = 16 * (jnp.arange(8, dtype=jnp.int32) % 4)[:, None] + jnp.arange(16, dtype=jnp.int32)
    owner = (jnp.arange(8, dtype=jnp.int32) // 4)[:, None]
    lists = []
    for source in (core, 1 - core):
        found = match & (owner == source)[:, :, None]
        first = jnp.min(jnp.where(found, entry[:, :, None], 64), axis=(1, 2))
        last = jnp.max(jnp.where(found, entry[:, :, None], -1), axis=(1, 2))
        lists.append(first)
        lists.append(jnp.where(last > first, last, 64))
    bwd_idx = jnp.concatenate(lists, axis=1)

    f32 = jnp.float32

    def vmem(*shape):
        return pltpu.VMEM(shape, f32)

    any_spec = pl.BlockSpec(memory_space=pl.ANY)
    smem_spec = pl.BlockSpec(memory_space=pltpu.SMEM)
    block = (32, 128)
    return pl.pallas_call(
        kernel,
        out_shape=jax.ShapeDtypeStruct((4, 4, 32, 128), f32),
        in_specs=[smem_spec, smem_spec, any_spec, any_spec, any_spec],
        out_specs=pl.BlockSpec(memory_space=pltpu.VMEM),
        scratch_shapes=[
            vmem(4, 4, 128, 128),
            vmem(4, 4, 4, *block),
            vmem(3, 4, 512, 128),
            pltpu.VMEM((4, 128, 512), jnp.bfloat16),
            pltpu.VMEM((4, 128, 512), jnp.bfloat16),
            vmem(4, 4, *block),
            vmem(4, *block),
            vmem(256, *block),
            vmem(256, *block),
            vmem(256, *block),
            vmem(3, 4, 4, *block),
            vmem(3, 3, 4, *block),
            vmem(4, 4, 4, *block),
            vmem(4, 128, 128),
            vmem(65, *block),
            vmem(65, *block),
            vmem(65, *block),
            vmem(65, *block),
            vmem(65, *block),
            vmem(65, *block),
            vmem(3, 128, *block),
            vmem(3, 4, 4, 2, *block),
            vmem(3, 4, 4, 2, *block),
            vmem(3, 4, 2, *block),
            vmem(3, 3, 2, *block),
            vmem(3, 16, *block),
            vmem(3, 16, *block),
            vmem(3, 16, *block),
            vmem(3, 16, *block),
            vmem(3, 16, *block),
            vmem(3, 7, 2, *block),
            pltpu.SemaphoreType.DMA((4,)),
            pltpu.SemaphoreType.DMA((8,)),
            pltpu.SemaphoreType.DMA((4, 3)),
            pltpu.SemaphoreType.DMA((3, 96)),
            pltpu.SemaphoreType.DMA((3, 96)),
            pltpu.SemaphoreType.DMA((7, 2, 3)),
        ],
        compiler_params=pltpu.CompilerParams(
            collective_id=0, has_side_effects=True, vmem_limit_bytes=60 * 1024 * 1024
        ),
    )(fwd_idx, bwd_idx, right_sides, inverse_diag, lower_blocks.reshape(3, 4, 512, 128))


def solution(mesh):
    return jax.shard_map(
        on_device,
        mesh=mesh,
        in_specs=(
            P(None, "row", None, None),
            P(None, "row", "col", None),
            P(None, "row", None, "col", None),
            P(),
        ),
        out_specs=P(None, "row", "col", None),
        check_vma=False,
    )
```
